512 devices in a mesh: docs: 64 (over x, z_lo, core), blk: 8 (over y, z_hi).
Axes of the slice: x: 4, y: 4, z: 16 (z_hi: 2, z_lo: 8; z = z_hi * 8 + z_lo), core: 2. Of those that a mesh axis runs over, the one named last changes fastest.
Arguments:
- group_rows: bfloat16 [8, 16384, 2048], P('blk', 'docs'), may hold values from -0.14941406 to 0.14941406
- group_owner: int32 [8, 16384, 1], P('blk', 'docs'), may hold values from 0 to 63; in each aligned block of 256 rows (0 to 255, 256 to 511, ..., all dimensions but the last counted through in order) at most 8 rows name the same one
- group_doc: int32 [8, 16384], P('blk', 'docs'), may hold values from 0 to 255
- doc_weight: float32 [8, 16384], P('blk', 'docs'), may hold values from 0.1 to 1
- queries: bfloat16 [256, 2048], P('blk'), may hold values from -6 to 6
- precond: bfloat16 [2048, 2048], P(None, 'docs'), may hold values from -0.125 to 0.125
Outputs:
- scores: float32 [256, 8, 16384], P(None, 'blk', 'docs')
The draws below stay inside these ranges and needn't reach their ends.
Inputs may be any that keep to these rules, and one draw needn't show every extreme that they name: `group_owner`: within the rows of one device, at most 8 groups name the same owner, and some owner gets exactly 8.
All inputs are finite; a program needn't handle non-finite values.
Results may differ from the reference program's by a relative error of at most 0.006.
Values may be sent and summed in bfloat16 or wider, within the bound.
A program may use at most 64 MiB of HBM per device.

```python
import math
import jax
import jax.numpy as jnp
import numpy as np
from jax import lax

K = 2048
DOC_DEV = 256
GROUP_DEV = 256
PEERS = 64
BLOCKS = 8
CAP = 8
QUERIES = 256
DOCS_COL = 16384
GROUPS_COL = 16384


def place_ends(drawn, rng, smallest, top_value):
    longest = drawn.shape.index(max(drawn.shape))
    spots = []
    for shift in (0, 1):
        where = [jax.random.randint(jax.random.fold_in(rng, axis), (), 0, length) for axis, length in enumerate(drawn.shape)]
        where[longest] = (where[longest] + shift) % drawn.shape[longest]
        spots.append(tuple(where))
    return drawn.at[spots[0]].set(smallest).at[spots[1]].set(top_value)


def steps_of(own_key, shape, split, least, top_value):
    factor_of, own = 1.0, jax.random.fold_in(own_key, 6)
    for position, blocks in split:
        heights = jnp.exp(jax.random.uniform(jax.random.fold_in(own, position), (blocks,), jnp.float32, least / len(split), top_value / len(split)))
        factor_of = factor_of * jnp.repeat(heights, shape[position] // blocks).reshape([-1 if axis == position else 1 for axis in range(len(shape))])
    return factor_of


def shared_out(key, own, number, rows, count, top, reach, skew):
    ranking = jax.random.permutation(key, count)
    crowded, common = portions_of(count, rows * top, reach, skew, True), portions_of(count, rows * top, reach, skew, False)
    places = jnp.arange(count)

    def named(lengths, turn):
        used = int((lengths > 0).sum())
        fixed = max(1, used // 4)
        moved = fixed + (places - fixed + turn * (used - fixed)) % max(1, count - fixed)
        return jnp.zeros((count,), jnp.int32).at[ranking[jnp.where(places < fixed, places, moved)]].set(jnp.asarray(lengths, jnp.int32))

    lengths = jnp.where(number % 4 == 0, named(crowded, number // 4), named(common, number - number // 4 - 1))
    mixed = jax.random.permutation(jax.random.fold_in(own, 3), count)
    giver, sink = mixed[0:count // 2 * 2:2], mixed[1:count // 2 * 2:2]
    margin = jnp.minimum(lengths[giver] - 1, reach - lengths[sink]) // 2
    margin = jnp.where((giver == ranking[0]) | (sink == ranking[0]) | (lengths[sink] == 0), 0, jnp.maximum(margin, 0))
    moved = jax.random.randint(jax.random.fold_in(own, 4), (count // 2,), 0, 1 << 20) % (margin + 1)
    lengths = lengths.at[giver].add(-moved).at[sink].add(moved)
    members = jnp.searchsorted(jnp.cumsum(lengths), jnp.arange(rows * top), side="right").astype(jnp.int32)
    table = members.reshape(top, rows).T
    table = table[jax.random.permutation(jax.random.fold_in(own, 1), rows)]
    turn = jax.random.randint(jax.random.fold_in(own, 2), (rows, 1), 0, top)
    return jnp.take_along_axis(table, (jnp.arange(top)[None, :] + turn) % top, axis=1)


def portions_of(number_of, total, bound, skew, full):
    loads = [(1 << 20) // math.isqrt(standing ** skew) + 1 for standing in range(1, number_of + 1)]
    largest = bound if full else min(bound, max(-(-total // number_of), total * loads[0] // sum(loads)))
    least = 1 if total - largest >= number_of - 1 else 0
    holding, surplus = [largest] + [least] * (number_of - 1), total - largest - least * (number_of - 1)
    while surplus > 0:
        movable = [i for i in range(1, number_of) if holding[i] < largest] or [i for i in range(1, number_of) if holding[i] < bound]
        pool, budget = sum([loads[i] for i in movable]), surplus
        for i in movable:
            addition = min(bound - holding[i], max(1, budget * loads[i] // pool), surplus)
            holding[i] = holding[i] + addition
            surplus = surplus - addition
    return np.array(holding)


def centred(key, extent, spread, most, shards=(), dtype=jnp.bfloat16):
    drawn = spread * jax.random.normal(key, extent, jnp.float32)
    if shards:
        drawn = drawn * steps_of(key, extent, shards, -0.22, 0.18)
    return jnp.clip(drawn, -most, most).astype(dtype)


def setup_inputs(seed: int = 0) -> dict:
    key_of = jax.random.split(jax.random.key(seed), 7)
    group_rows = centred(key_of[0], (BLOCKS, GROUPS_COL, K), 0.022, 0.14941406, ((0, 8), (1, 64)))
    group_owner_keys = jax.random.split(jax.random.fold_in(key_of[1], 1), BLOCKS * GROUPS_COL // GROUP_DEV)
    group_owner_turns = jax.random.permutation(jax.random.fold_in(key_of[1], 3), BLOCKS * GROUPS_COL // GROUP_DEV)
    group_owner = jax.vmap(lambda own, number: shared_out(jax.random.fold_in(key_of[1], 2), own, number, GROUP_DEV, PEERS, 1, CAP, 2))(group_owner_keys, group_owner_turns).reshape((BLOCKS, GROUPS_COL, 1))
    group_doc = place_ends(jax.random.randint(key_of[2], (BLOCKS, GROUPS_COL), 0, DOC_DEV), jax.random.fold_in(key_of[2], 1), 0, DOC_DEV - 1).astype(jnp.int32)
    doc_weight = jnp.clip(0.1 + 0.9 * jax.random.uniform(key_of[3], (BLOCKS, DOCS_COL), jnp.float32) ** steps_of(key_of[3], (BLOCKS, DOCS_COL), ((0, 8), (1, 64)), -0.2, 0.2), 0.1, 1.0)
    queries = centred(key_of[4], (QUERIES, K), 1.0, 6.0, ((0, 8),))
    precond = centred(key_of[5], (K, K), K ** -0.5, 0.125, ((1, 64),))
    return dict(group_rows=group_rows, group_owner=group_owner, group_doc=group_doc, doc_weight=doc_weight, queries=queries, precond=precond)


def reference(group_rows, group_owner, group_doc, doc_weight, queries, precond):
    target = (group_owner[:, :, 0] * DOC_DEV + group_doc).astype(jnp.int32)

    def column(args):
        rows, ids = args
        return jax.ops.segment_sum(rows.astype(jnp.float32), ids, num_segments=DOCS_COL)

    doc_print = lax.map(column, (group_rows, target))
    query_pre = jnp.dot(queries, precond, preferred_element_type=jnp.float32).astype(jnp.bfloat16)
    query_wide = query_pre.astype(jnp.float32)

    def score_column(args):
        prints, weight = args
        product = jnp.dot(query_wide, prints.T, precision=lax.Precision.HIGHEST, preferred_element_type=jnp.float32)
        return product * weight[None, :]

    per_column = lax.map(score_column, (doc_print, doc_weight))
    return jnp.transpose(per_column, (1, 0, 2))
```

```python
import jax
import jax.numpy as jnp
from jax import lax
from jax.sharding import PartitionSpec as P

NT = (((1,), (1,)), ((), ()))


def shards(group_rows, group_owner, group_doc, doc_weight, queries, precond):
    rows = group_rows[0]
    owner = group_owner[0, :, 0]
    doc_index = group_doc[0]
    peers = lax.axis_size("docs")
    count = rows.shape[0]
    capacity = 2 * count // peers
    slots = peers * capacity
    peer_ids = jnp.arange(peers, dtype=jnp.int32)
    owner_table = (peer_ids[:, None] == owner[None, :])
    order = jnp.arange(count, dtype=jnp.int32)
    before = (order[:, None] < order[None, :]).astype(jnp.bfloat16)
    earlier = jnp.dot(owner_table.astype(jnp.bfloat16), before, preferred_element_type=jnp.float32)
    rank = jnp.sum(jnp.where(owner_table, earlier, 0.0), axis=0).astype(jnp.int32)
    slot = owner * capacity + rank
    pick = jnp.arange(slots, dtype=jnp.int32)[:, None] == slot[None, :]
    send_ids = jnp.max(jnp.where(pick, doc_index[None, :], -1), axis=1).reshape(peers, capacity)
    got_ids = lax.all_to_all(send_ids, "docs", split_axis=0, concat_axis=0, tiled=True).reshape(slots)
    query_pre = jnp.dot(queries, precond, preferred_element_type=jnp.float32).astype(jnp.bfloat16)
    full_rows = lax.all_gather(query_pre, "docs", axis=1, tiled=True)
    full = lax.all_gather(full_rows, "blk", axis=0, tiled=True)
    part = lax.dot_general(rows, full, NT, preferred_element_type=jnp.float32).astype(jnp.bfloat16)
    send = jnp.dot(pick.astype(jnp.bfloat16), part, preferred_element_type=jnp.float32).astype(jnp.bfloat16)
    send = send.reshape(peers, capacity, send.shape[1])
    got = lax.all_to_all(send, "docs", split_axis=0, concat_axis=0, tiled=True)
    got = got.reshape(slots, got.shape[2])
    doc_ids = jnp.arange(doc_weight.shape[1], dtype=jnp.int32)
    member = (got_ids[:, None] == doc_ids[None, :]).astype(jnp.bfloat16)
    scores = lax.dot_general(got, member, (((0,), (0,)), ((), ())), preferred_element_type=jnp.float32)
    return (scores * doc_weight[0][None, :])[:, None, :]


def solution(mesh):
    return jax.shard_map(
        shards,
        mesh=mesh,
        in_specs=(
            P("blk", "docs", None),
            P("blk", "docs", None),
            P("blk", "docs"),
            P("blk", "docs"),
            P("blk", None),
            P(None, "docs"),
        ),
        out_specs=P(None, "blk", "docs"),
        check_vma=False,
    )
```

```python
import functools

import jax
import jax.numpy as jnp
from jax import lax
from jax.experimental import pallas as pl
from jax.experimental.pallas import tpu as pltpu
from jax.sharding import PartitionSpec as P

X, Y, Z_LO, Z_HI = 4, 4, 8, 2
MESH = pl.DeviceIdType.MESH
NT = (((1,), (1,)), ((), ()))
TN = (((0,), (0,)), ((), ()))
F32, BF16 = jnp.float32, jnp.bfloat16


def dot(a, b, dims):
    return lax.dot_general(a, b, dims, preferred_element_type=F32)


def iota(shape, axis):
    return lax.broadcasted_iota(jnp.int32, shape, axis)


def kernel(
    rows_hbm, owner_ref, doc_ref, query_hbm, pre_hbm, out_ref,
    rows, owner2, doc2, query, pre, half, swapped, ztile, gathered, pick,
    id_send, id_got, send, got, member, result,
    loc_sem, sw_s, sw_r, za_s, za_r, zb_s, zb_r, x_s, x_r, y_s, y_r,
    i_s, i_r, a_s, a_r, o_s, o_r,
):
    zn = Z_LO * Z_HI
    reach = zn // 4
    chips = X * Z_LO
    count = rows.shape[1]
    owners = 2 * chips
    cap = 2 * count // owners
    d, b = lax.axis_index("docs"), lax.axis_index("blk")
    core, chip = d % 2, d // 2
    x, z_lo = chip // Z_LO, chip % Z_LO
    y, z_hi = b // Z_HI, b % Z_HI
    z = z_hi * Z_LO + z_lo

    def at(dx=0, dy=0, dz=0, other=False):
        nx, ny, nz = (x + dx) % X, (y + dy) % Y, (z + dz + zn) % zn
        nc = 1 - core if other else core
        return {"docs": (nx * Z_LO + nz % Z_LO) * 2 + nc, "blk": ny * Z_HI + nz // Z_LO}

    def remote(src, dst, s, r, device):
        return pltpu.make_async_remote_copy(
            src_ref=src, dst_ref=dst, send_sem=s, recv_sem=r, device_id=device, device_id_type=MESH
        )

    load_query = pltpu.make_async_copy(query_hbm, query, loc_sem.at[0])
    load_pre = pltpu.make_async_copy(pre_hbm, pre, loc_sem.at[1])
    load_rows = pltpu.make_async_copy(rows_hbm, rows.at[0], loc_sem.at[2])
    load_query.start()
    load_pre.start()
    load_rows.start()

    partners = [at(other=True)]
    for j in range(1, reach + 1):
        partners += [at(dz=j), at(dz=-j)]
    partners += [at(dx=j) for j in range(1, X)] + [at(dy=j) for j in range(1, Y)]
    barrier = pltpu.get_barrier_semaphore()
    for device in partners:
        pl.semaphore_signal(barrier, inc=1, device_id=device, device_id_type=MESH)

    load_query.wait()
    load_pre.wait()
    wide = jnp.concatenate([pre[...]] * 4, axis=0)
    block = dot(query[...], wide, NT)
    keep = iota(block.shape, 1) // 32 == d % 4
    block = jnp.where(keep, block, 0.0).astype(BF16)
    half[...] = block.reshape(half.shape)

    pl.semaphore_wait(barrier, len(partners))

    swaps = [
        remote(half.at[1 - core], swapped, sw_s.at[0], sw_r.at[0], at(other=True)),
        remote(owner_ref, owner2, sw_s.at[1], sw_r.at[1], at(other=True)),
        remote(doc_ref, doc2, sw_s.at[2], sw_r.at[2], at(other=True)),
        remote(rows_hbm, rows.at[1], sw_s.at[3], sw_r.at[3], at(other=True)),
    ]
    for copy in swaps:
        copy.start()
    swaps[0].wait()
    ztile[z] = half[core] + swapped[...]
    own_tile = ztile.at[z]
    near = {}
    for j in range(reach, 0, -1):
        for k, dz in ((2 * j - 2, j), (2 * j - 1, -j)):
            near[dz] = remote(own_tile, own_tile, za_s.at[k], za_r.at[k], at(dz=dz))
            near[dz].start()

    swaps[1].wait()
    swaps[2].wait()
    slots = owners * 2 * cap
    before = (iota((count, count), 0) < iota((count, count), 1)).astype(BF16)
    id_table = jnp.zeros((chips, 128), F32)
    for side in range(2):
        owner_row = (owner_ref if side == 0 else owner2)[...]
        doc_row = (doc_ref if side == 0 else doc2)[...]
        table = iota((owners, count), 0) == owner_row
        earlier = dot(table.astype(BF16), before, (((1,), (0,)), ((), ())))
        rank = jnp.sum(jnp.where(table, earlier, 0.0), axis=0, keepdims=True).astype(jnp.int32)
        source = core if side == 0 else 1 - core
        lane = (owner_row % 2) * (2 * cap) + source * cap + rank
        to_chip = owner_row // 2
        slot = to_chip * (4 * cap) + lane
        pick[:, side * count:(side + 1) * count] = (iota((slots, count), 0) == slot).astype(BF16)
        doc_one = (doc_row + 1).astype(F32)
        chip_side = jnp.where(iota((chips, count), 0) == to_chip, doc_one, 0.0).astype(BF16)
        lane_side = (iota((128, count), 0) == lane).astype(BF16)
        id_table = id_table + dot(chip_side, lane_side, NT)
    id_send[...] = id_table.reshape(id_send.shape)

    far = []
    for j in range(1, reach + 1):
        for k, dz in ((2 * j - 2, j), (2 * j - 1, -j)):
            near[dz].wait_recv()
            if dz == -reach:
                continue
            tile = ztile.at[(z - dz + zn) % zn]
            copy = remote(tile, tile, zb_s.at[k], zb_r.at[k], at(dz=reach if dz > 0 else -reach))
            copy.start()
            far.append(copy)
    for copy in far:
        copy.wait_recv()

    for hi in range(Z_HI):
        for p in range(Z_LO // 2):
            first = hi * Z_LO + 2 * p
            gathered[y, x, hi * 16:(hi + 1) * 16, p * 128:(p + 1) * 128] = ztile[first] + ztile[first + 1]
    own_piece = gathered.at[y, x]
    across = []
    for j in range(1, X):
        copy = remote(own_piece, own_piece, x_s.at[j - 1], x_r.at[j - 1], at(dx=j))
        copy.start()
        across.append(copy)
    along = []
    for i in range(X):
        if i:
            across[i - 1].wait_recv()
        piece = gathered.at[y, (x - i + X) % X]
        for j in range(1, Y):
            copy = remote(piece, piece, y_s.at[j - 1, i], y_r.at[j - 1, i], at(dy=j))
            copy.start()
            along.append(copy)

    def to(i):
        other = (chip + i) % chips
        return other, {"docs": other * 2 + core, "blk": b}

    def id_copy(i):
        other, device = to(i)
        return remote(id_send.at[other], id_got.at[chip], i_s.at[i], i_r.at[i], device)

    def score_copy(i):
        other, device = to(i)
        return remote(send.at[other], got.at[chip], a_s.at[i], a_r.at[i], device)

    def each(fn):
        lax.fori_loop(1, chips, lambda i, c: (fn(i), c)[1], 0)

    each(lambda i: id_copy(i).start())
    own_ids = pltpu.make_async_copy(id_send.at[chip], id_got.at[chip], loc_sem.at[3])
    own_ids.start()
    load_rows.wait()
    swaps[3].wait()
    for copy in along:
        copy.wait_recv()

    part = None
    span = gathered.shape[3]
    for i in range(X):
        left = rows[:, :, i * span:(i + 1) * span].reshape(2 * count, span)
        right = gathered[:, i].reshape(Y * gathered.shape[2], span)
        term = dot(left, right, NT)
        part = term if part is None else part + term
    packed = dot(pick[...], part.astype(BF16), (((1,), (0,)), ((), ()))).astype(BF16)
    send[...] = packed.reshape(send.shape)

    each(lambda i: score_copy(i).start())
    own_scores = pltpu.make_async_copy(send.at[chip], got.at[chip], loc_sem.at[4])
    own_scores.start()

    own_ids.wait()
    each(lambda i: id_copy(i).wait_recv())
    per = chips * 2 * cap
    spread = (iota((per, chips), 0) // (2 * cap) == iota((per, chips), 1)).astype(BF16)
    ids = dot(spread, id_got[...].reshape(chips, 128).astype(BF16), (((1,), (0,)), ((), ())))
    for e in range(2):
        mine = iota(ids.shape, 1) == e * 2 * cap + iota(ids.shape, 0) % (2 * cap)
        column = jnp.sum(jnp.where(mine, ids, 0.0), axis=1, keepdims=True).astype(jnp.int32) - 1
        member[e] = (column == iota((per, member.shape[2]), 1)).astype(BF16)

    own_scores.wait()
    each(lambda i: score_copy(i).wait_recv())
    for e in (1 - core, core):
        total = dot(got[:, e].reshape(per, got.shape[3]), member[e], TN)
        shape = (out_ref.shape[0],) + out_ref.shape[2:]
        if e is core:
            out_ref[:, core] = total.reshape(shape)
        else:
            result[...] = total.reshape(shape)
            give = remote(result, out_ref.at[:, core], o_s, o_r, at(other=True))
            give.start()
    give.wait()

    for copy in list(near.values()) + far + across + along:
        copy.wait_send()
    each(lambda i: id_copy(i).wait_send())
    each(lambda i: score_copy(i).wait_send())


def shards(group_rows, group_owner, group_doc, doc_weight, queries, precond):
    rows = group_rows[0]
    count, width = rows.shape
    docs, blks = lax.axis_size("docs"), lax.axis_size("blk")
    chips, zn = X * Z_LO, Z_LO * Z_HI
    reach = zn // 4
    cap = 2 * count // docs
    own_q, part = queries.shape[0], precond.shape[1]
    doc_count = doc_weight.shape[1]
    lanes = Y * Z_HI * own_q // 2
    dma = pltpu.SemaphoreType.DMA
    any_spec = pl.BlockSpec(memory_space=pl.ANY)
    vmem = pl.BlockSpec(memory_space=pltpu.VMEM)
    total = pl.pallas_call(
        kernel,
        out_shape=jax.ShapeDtypeStruct((blks, 2, own_q // 2, doc_count), F32),
        in_specs=[any_spec, vmem, vmem, any_spec, any_spec],
        out_specs=vmem,
        scratch_shapes=[
            pltpu.VMEM((2, count, width), BF16),
            pltpu.VMEM((1, count), jnp.int32),
            pltpu.VMEM((1, count), jnp.int32),
            pltpu.VMEM(queries.shape, BF16),
            pltpu.VMEM((part, width), BF16),
            pltpu.VMEM((2, own_q // 2, 128), BF16),
            pltpu.VMEM((own_q // 2, 128), BF16),
            pltpu.VMEM((zn, own_q // 2, 128), BF16),
            pltpu.VMEM((Y, X, Z_HI * own_q // 2, width // X), BF16),
            pltpu.VMEM((docs * 2 * cap, 2 * count), BF16),
            pltpu.VMEM((chips, 1, 128), F32),
            pltpu.VMEM((chips, 1, 128), F32),
            pltpu.VMEM((chips, 2, 2 * cap, lanes), BF16),
            pltpu.VMEM((chips, 2, 2 * cap, lanes), BF16),
            pltpu.VMEM((2, chips * 2 * cap, doc_count), BF16),
            pltpu.VMEM((blks, own_q // 2, doc_count), F32),
            dma((5,)), dma((4,)), dma((4,)),
            dma((2 * reach,)), dma((2 * reach,)), dma((2 * reach,)), dma((2 * reach,)),
            dma((max(X - 1, 1),)), dma((max(X - 1, 1),)),
            dma((max(Y - 1, 1), X)), dma((max(Y - 1, 1), X)),
            dma((chips,)), dma((chips,)), dma((chips,)), dma((chips,)),
            dma, dma,
        ],
        compiler_params=pltpu.CompilerParams(collective_id=0, has_side_effects=True),
    )(rows, group_owner.reshape(1, count), group_doc, queries, precond.T)
    scores = total.reshape(blks * own_q, doc_count) * doc_weight[0][None, :]
    return scores[:, None, :]


def solution(mesh):
    return jax.shard_map(
        shards,
        mesh=mesh,
        in_specs=(
            P("blk", "docs", None),
            P("blk", "docs", None),
            P("blk", "docs"),
            P("blk", "docs"),
            P("blk", None),
            P(None, "docs"),
        ),
        out_specs=P(None, "blk", "docs"),
        check_vma=False,
    )
```

```python
import jax
import jax.numpy as jnp
from jax import lax
from jax.experimental import pallas as pl
from jax.experimental.pallas import tpu as pltpu
from jax.sharding import PartitionSpec as P

X, Y, Z_LO, Z_HI = 4, 4, 8, 2
MESH = pl.DeviceIdType.MESH
NN = (((1,), (0,)), ((), ()))
NT = (((1,), (1,)), ((), ()))
TN = (((0,), (0,)), ((), ()))
F32, BF16 = jnp.float32, jnp.bfloat16


def dot(a, b, dims):
    return lax.dot_general(a, b, dims, preferred_element_type=F32)


def iota(shape, axis):
    return lax.broadcasted_iota(jnp.int32, shape, axis)


def kernel(
    rows_hbm, owner_hbm, doc_hbm, weight_hbm, query_hbm, pre_hbm, out_ref,
    rows, owner, doc, weight, query, pre, mine, tiles, gathered, pick,
    id_send, id_got, send, got,
    loc_sem, go_sem, sw_s, sw_r, z_s, z_r, x_s, x_r, y_s, y_r, p_s, p_r,
    i_s, i_r, a_s, a_r,
):
    chips = X * Z_LO
    count = rows.shape[1]
    owners = 2 * chips
    cap = 2 * count // owners
    d, b = lax.axis_index("docs"), lax.axis_index("blk")
    core, chip = d % 2, d // 2
    x, z_lo = chip // Z_LO, chip % Z_LO
    y, z_hi = b // Z_HI, b % Z_HI
    native = core == z_hi
    low = z_hi == 0

    def at(dx=0, dy=0, lo=None, hi=None, c=None):
        lo, hi, c = (z_lo if lo is None else lo), (z_hi if hi is None else hi), (core if c is None else c)
        return {"docs": ((x + dx) % X * Z_LO + lo) * 2 + c, "blk": (y + dy) % Y * Z_HI + hi}

    def remote(src, dst, s, r, device):
        return pltpu.make_async_remote_copy(
            src_ref=src, dst_ref=dst, send_sem=s, recv_sem=r, device_id=device, device_id_type=MESH
        )

    barrier = pltpu.get_barrier_semaphore()

    def greet(device):
        pl.semaphore_signal(barrier, inc=1, device_id=device, device_id_type=MESH)

    for j in range(1, X):
        greet(at(dx=j))
    for j in range(1, Y):
        greet(at(dy=j))
    partner = at(c=1 - core)

    @pl.when(native)
    def _():
        greet(partner)
        for o in range(1, Z_LO):
            for c in range(2):
                greet(at(lo=(z_lo + o) % Z_LO, c=c))

    @pl.when(jnp.logical_not(native))
    def _():
        greet(partner)

    @pl.when(jnp.logical_and(low, native))
    def _():
        greet(at(hi=1))

    @pl.when(jnp.logical_and(low, jnp.logical_not(native)))
    def _():
        for o in range(Z_LO):
            for c in range(2):
                greet(at(lo=(z_lo + o) % Z_LO, hi=1, c=c))

    loads = [
        pltpu.make_async_copy(src, dst, loc_sem.at[i])
        for i, (src, dst) in enumerate(
            [
                (query_hbm, query), (pre_hbm, pre), (rows_hbm, rows.at[core]),
                (owner_hbm, owner.at[core]), (doc_hbm, doc.at[core]), (weight_hbm, weight),
            ]
        )
    ]
    for copy in loads:
        copy.start()

    loads[0].wait()
    loads[1].wait()
    block = dot(query[...], jnp.concatenate([pre[...]] * 4, axis=0), NT)
    group = iota((8, 128), 1) // 32
    tile = jnp.zeros((8, 128), F32)
    for j in range(4):
        tile = jnp.where(group == j, block[8 * j:8 * j + 8], tile)
    tile = tile.astype(BF16)
    mine[...] = tile

    def place(lo, c):
        return tiles.at[lo % 2 * 2 + c, lo // 2]

    @pl.when(native)
    def _():
        tiles[z_lo % 2 * 2 + core, z_lo // 2] = tile

    few = 2 * X + 2 * Y - 2 - (X + Y) + Z_LO
    many = few + Z_LO
    pl.semaphore_wait(barrier, jnp.where(low, few, many + jnp.where(native, 0, 1)))

    def tile_copy(o, hi, c=None):
        return remote(
            mine, place(z_lo, core), z_s.at[hi, o], z_r.at[o, core], at(lo=(z_lo + o) % Z_LO, hi=hi, c=z_hi)
        )

    def tile_wait(o, c):
        remote(mine, place((z_lo - o + Z_LO) % Z_LO, c), z_s.at[0, 0], z_r.at[o, c], partner).wait_recv()

    high = jnp.logical_not(low)

    @pl.when(high)
    def _():
        for o in range(Z_LO):
            tile_copy(o, 0).start()

    for o in range(Z_LO - 1, 0, -1):
        tile_copy(o, z_hi).start()

    @pl.when(jnp.logical_not(native))
    def _():
        tile_copy(0, z_hi).start()

    def go(device):
        pl.semaphore_signal(go_sem, inc=1, device_id=device, device_id_type=MESH)

    @pl.when(jnp.logical_and(high, jnp.logical_not(native)))
    def _():
        go(at(hi=0))

    loads[3].wait()
    loads[4].wait()
    swaps = [
        remote(owner.at[core], owner.at[core], sw_s.at[0], sw_r.at[0], partner),
        remote(doc.at[core], doc.at[core], sw_s.at[1], sw_r.at[1], partner),
        remote(rows_hbm, rows.at[core], sw_s.at[2], sw_r.at[2], partner),
    ]
    for copy in swaps:
        copy.start()

    swaps[0].wait()
    swaps[1].wait()
    before = (iota((count, count), 0) < iota((count, count), 1)).astype(BF16)
    id_table = jnp.zeros((owners, 128), F32)
    for side in range(2):
        owner_row = owner[side]
        table = iota((owners, count), 0) == owner_row
        earlier = dot(table.astype(BF16), before, NN)
        rank = jnp.sum(jnp.where(table, earlier, 0.0), axis=0, keepdims=True).astype(jnp.int32)
        slot = owner_row * cap + rank
        pick[side] = (iota((owners * cap, count), 0) == slot).astype(BF16)
        doc_side = jnp.where(table, (doc[side] + 1).astype(F32), 0.0).astype(BF16)
        lane_side = (iota((128, count), 0) == side * cap + rank).astype(BF16)
        id_table = id_table + dot(doc_side, lane_side, NT)
    id_send[...] = id_table.reshape(id_send.shape)
    n = 4 * 128
    row, col = iota((n, n), 0), iota((n, n), 1)
    turn = (row // 128 == col % 128 // 32) & (row % 128 // 32 == col // 128) & (row % 32 == col % 32)
    turn = turn.astype(BF16)

    own_piece = gathered.at[y, x]
    over = remote(own_piece, own_piece, p_s, p_r, at(hi=1))
    by_piece = jnp.logical_and(high, jnp.logical_not(native))

    @pl.when(by_piece)
    def _():
        over.wait_recv()

    @pl.when(jnp.logical_not(by_piece))
    def _():
        @pl.when(jnp.logical_not(native))
        def _():
            tile_wait(0, 0)
            tile_wait(0, 1)

        @pl.when(native)
        def _():
            tile_wait(0, 1 - core)

        for o in range(1, Z_LO):
            for c in range(2):
                tile_wait(o, c)
        left = [tiles[i].astype(F32).reshape(Z_LO // 2 * 8, 128).astype(BF16) for i in range(4)]
        mixed = dot(jnp.concatenate(left, axis=1), turn, NN)
        for p in range(Z_LO // 2):
            part = [mixed[8 * p:8 * p + 8, 128 * j:128 * j + 128] for j in range(4)]
            gathered[y, x, :, 128 * p:128 * p + 128] = jnp.concatenate(part, axis=0).astype(BF16)

    across, along = [], []
    for j in range(1, X):
        across.append(remote(own_piece, own_piece, x_s.at[j - 1], x_r.at[j - 1], at(dx=j)))
        across[-1].start()
    for i in range(X):
        if i:
            across[i - 1].wait_recv()
        piece = gathered.at[y, (x - i + X) % X]
        for j in range(1, Y):
            along.append(remote(piece, piece, y_s.at[j - 1, i], y_r.at[j - 1, i], at(dy=j)))
            along[-1].start()
        if i == min(1, X - 1):
            @pl.when(jnp.logical_and(low, native))
            def _():
                pl.semaphore_wait(go_sem, 1)
                over.start()

    def target(t):
        other = (chip + t // 2) % chips * 2 + t % 2
        return other, {"docs": other, "blk": b}

    def id_copy(t):
        other, device = target(t)
        return remote(id_send.at[other], id_got.at[chip], i_s.at[t], i_r.at[t // 2], device)

    def score_copy(t):
        other, device = target(t)
        return remote(send.at[other], got.at[core, chip], a_s.at[t], a_r.at[core, t // 2], device)

    def score_wait(c, i):
        remote(send.at[0], got.at[c, (chip - i + chips) % chips], a_s.at[0], a_r.at[c, i], partner).wait_recv()

    def loop(start, stop, fn):
        lax.fori_loop(start, stop, lambda i, c: (fn(i), c)[1], 0)

    own_ids = pltpu.make_async_copy(id_send.at[d], id_got.at[chip], loc_sem.at[6])

    @pl.when(native)
    def _():
        loop(2, owners, lambda t: id_copy(t).start())
        id_copy(1 - core).start()
        own_ids.start()

    loads[2].wait()
    swaps[2].wait()
    for copy in along:
        copy.wait_recv()

    span = gathered.shape[3]
    packed = []
    for side in range(2):
        part = None
        for i in range(X):
            term = dot(rows[side, :, i * span:(i + 1) * span], gathered[:, i].reshape(-1, span), NT)
            part = term if part is None else part + term
        packed.append(dot(pick[side], part.astype(BF16), NN).reshape(owners, cap, -1))
    send[...] = jnp.concatenate(packed, axis=1).astype(BF16)

    @pl.when(native)
    def _():
        own_ids.wait()

    @pl.when(jnp.logical_not(native))
    def _():
        id_copy(1 - core).wait_recv()

    loop(2, owners, lambda t: score_copy(t).start())
    score_copy(1 - core).start()
    own_scores = pltpu.make_async_copy(send.at[d], got.at[core, chip], loc_sem.at[7])
    own_scores.start()

    loop(1, chips, lambda i: id_copy(2 * i).wait_recv())
    per = chips * 2 * cap
    spread = (iota((per, chips), 0) // (2 * cap) == iota((per, chips), 1)).astype(BF16)
    ids = dot(spread, id_got[...].reshape(chips, 128).astype(BF16), NN)
    keep = iota(ids.shape, 1) == iota(ids.shape, 0) % (2 * cap)
    column = jnp.sum(jnp.where(keep, ids, 0.0), axis=1, keepdims=True).astype(jnp.int32) - 1
    member = (column == iota((per, weight.shape[1]), 1)).astype(BF16)
    loads[5].wait()

    own_scores.wait()
    for first in range(2):
        c = z_hi if first == 0 else 1 - z_hi

        @pl.when(c != core)
        def _():
            score_wait(c, 0)

        loop(1, chips, lambda i: score_wait(c, i))
        total = dot(got[c].reshape(per, -1), member, TN) * weight[...]
        size = total.shape[0] // Y
        for k in range(Y):
            for nh in range(2):
                out_ref[k, c, pl.ds(nh, size, stride=2), :] = total[k * size:(k + 1) * size, nh * 128:nh * 128 + 128]

    @pl.when(high)
    def _():
        for o in range(Z_LO):
            tile_copy(o, 0).wait_send()

    for o in range(1, Z_LO):
        tile_copy(o, z_hi).wait_send()

    @pl.when(jnp.logical_not(native))
    def _():
        tile_copy(0, z_hi).wait_send()

    @pl.when(native)
    def _():
        loop(2, owners, lambda t: id_copy(t).wait_send())
        id_copy(1 - core).wait_send()

    @pl.when(jnp.logical_and(low, native))
    def _():
        over.wait_send()

    for copy in across + along:
        copy.wait_send()
    loop(2, owners, lambda t: score_copy(t).wait_send())
    score_copy(1 - core).wait_send()


def shards(group_rows, group_owner, group_doc, doc_weight, queries, precond):
    rows = group_rows[0]
    count, width = rows.shape
    docs, blks = lax.axis_size("docs"), lax.axis_size("blk")
    chips = X * Z_LO
    cap = 2 * count // docs
    own_q, part = queries.shape[0], precond.shape[1]
    doc_count = doc_weight.shape[1]
    dma = pltpu.SemaphoreType.DMA
    any_spec = pl.BlockSpec(memory_space=pl.ANY)
    vmem = pl.BlockSpec(memory_space=pltpu.VMEM)
    nx, ny = max(X - 1, 1), max(Y - 1, 1)
    total = pl.pallas_call(
        kernel,
        out_shape=jax.ShapeDtypeStruct((Y, 2, 2 * own_q, doc_count // 2), F32),
        in_specs=[any_spec] * 6,
        out_specs=vmem,
        scratch_shapes=[
            pltpu.VMEM((2, count, width), BF16),
            pltpu.VMEM((2, 1, count), jnp.int32),
            pltpu.VMEM((2, 1, count), jnp.int32),
            pltpu.VMEM((1, doc_count), F32),
            pltpu.VMEM(queries.shape, BF16),
            pltpu.VMEM((part, width), BF16),
            pltpu.VMEM((8, 128), BF16),
            pltpu.VMEM((4, Z_LO // 2, 8, 128), BF16),
            pltpu.VMEM((Y, X, own_q, width // X), BF16),
            pltpu.VMEM((2, docs * cap, count), BF16),
            pltpu.VMEM((docs, 1, 128), F32),
            pltpu.VMEM((chips, 1, 128), F32),
            pltpu.VMEM((docs, 2 * cap, Y * own_q), BF16),
            pltpu.VMEM((2, chips, 2 * cap, Y * own_q), BF16),
            dma((8,)), pltpu.SemaphoreType.REGULAR, dma((3,)), dma((3,)),
            dma((2, Z_LO)), dma((Z_LO, 2)), dma((nx,)), dma((nx,)), dma((ny, X)), dma((ny, X)), dma, dma,
            dma((docs,)), dma((chips,)), dma((docs,)), dma((2, chips)),
        ],
        compiler_params=pltpu.CompilerParams(collective_id=0, has_side_effects=True),
    )(rows, group_owner.reshape(1, count), group_doc, doc_weight, queries, precond.T)
    return total.reshape(blks * own_q, 1, doc_count)


def solution(mesh):
    return jax.shard_map(
        shards,
        mesh=mesh,
        in_specs=(
            P("blk", "docs", None),
            P("blk", "docs", None),
            P("blk", "docs"),
            P("blk", "docs"),
            P("blk", None),
            P(None, "docs"),
        ),
        out_specs=P(None, "blk", "docs"),
        check_vma=False,
    )
```

```python
import jax
import jax.numpy as jnp
from jax import lax
from jax.experimental import pallas as pl
from jax.experimental.pallas import tpu as pltpu
from jax.sharding import PartitionSpec as P

X, Y, Z_LO, Z_HI = 4, 4, 8, 2
MESH = pl.DeviceIdType.MESH
NN = (((1,), (0,)), ((), ()))
NT = (((1,), (1,)), ((), ()))
TN = (((0,), (0,)), ((), ()))
F32, BF16 = jnp.float32, jnp.bfloat16


def dot(a, b, dims):
    return lax.dot_general(a, b, dims, preferred_element_type=F32)


def iota(shape, axis):
    return lax.broadcasted_iota(jnp.int32, shape, axis)


def kernel(
    rows_hbm, owner_hbm, doc_hbm, weight_hbm, query_hbm, pre_hbm, out_ref,
    rows, owner, doc, weight, query, pre, mine, tiles, gathered, pick,
    id_send, id_got, send, got, before, turn,
    loc_sem, go_sem, sw_s, sw_r, z_s, z_r, f_s, f_r, g_s, g_r, p_s, p_r,
    i_s, i_r, a_s, a_r,
):
    chips = X * Z_LO
    count = rows.shape[1]
    owners = 2 * chips
    cap = 2 * count // owners
    d, b = lax.axis_index("docs"), lax.axis_index("blk")
    core, chip = d % 2, d // 2
    x, z_lo = chip // Z_LO, chip % Z_LO
    y, z_hi = b // Z_HI, b % Z_HI
    native = core == z_hi
    low = z_hi == 0

    def at(dx=0, dy=0, lo=None, hi=None, c=None):
        lo, hi, c = (z_lo if lo is None else lo), (z_hi if hi is None else hi), (core if c is None else c)
        return {"docs": ((x + dx) % X * Z_LO + lo) * 2 + c, "blk": (y + dy) % Y * Z_HI + hi}

    def remote(src, dst, s, r, device):
        return pltpu.make_async_remote_copy(
            src_ref=src, dst_ref=dst, send_sem=s, recv_sem=r, device_id=device, device_id_type=MESH
        )

    barrier = pltpu.get_barrier_semaphore()

    def greet(device):
        pl.semaphore_signal(barrier, inc=1, device_id=device, device_id_type=MESH)

    for j in range(1, X):
        greet(at(dx=j))
    for j in range(1, Y):
        greet(at(dy=j))
    partner = at(c=1 - core)

    @pl.when(native)
    def _():
        greet(partner)
        for o in range(1, Z_LO):
            for c in range(2):
                greet(at(lo=(z_lo + o) % Z_LO, c=c))

    @pl.when(jnp.logical_not(native))
    def _():
        greet(partner)

    @pl.when(jnp.logical_and(low, native))
    def _():
        greet(at(hi=1))

    @pl.when(jnp.logical_and(low, jnp.logical_not(native)))
    def _():
        for o in range(Z_LO):
            for c in range(2):
                greet(at(lo=(z_lo + o) % Z_LO, hi=1, c=c))

    loads = [
        pltpu.make_async_copy(src, dst, loc_sem.at[i])
        for i, (src, dst) in enumerate(
            [
                (query_hbm, query), (pre_hbm, pre), (rows_hbm, rows.at[core]),
                (owner_hbm, owner.at[core]), (doc_hbm, doc.at[core]), (weight_hbm, weight),
            ]
        )
    ]
    for copy in loads:
        copy.start()

    before[...] = (iota((count, count), 0) < iota((count, count), 1)).astype(BF16)
    n = 4 * 128
    row, col = iota((n, n), 0), iota((n, n), 1)
    placed = (row // 128 == col % 128 // 32) & (row % 128 // 32 == col // 128) & (row % 32 == col % 32)
    turn[...] = placed.astype(BF16)

    loads[0].wait()
    loads[1].wait()
    block = dot(query[...], jnp.concatenate([pre[...]] * 4, axis=0), NT)
    group = iota((8, 128), 1) // 32
    tile = jnp.zeros((8, 128), F32)
    for j in range(4):
        tile = jnp.where(group == j, block[8 * j:8 * j + 8], tile)
    tile = tile.astype(BF16)
    mine[...] = tile

    def place(lo, c):
        return tiles.at[lo % 2 * 2 + c, lo // 2]

    @pl.when(native)
    def _():
        tiles[z_lo % 2 * 2 + core, z_lo // 2] = tile

    few = 2 * X + 2 * Y - 2 - (X + Y) + Z_LO
    many = few + Z_LO
    pl.semaphore_wait(barrier, jnp.where(low, few, many + jnp.where(native, 0, 1)))

    def tile_copy(o, hi, c=None):
        return remote(
            mine, place(z_lo, core), z_s.at[hi, o], z_r.at[o, core], at(lo=(z_lo + o) % Z_LO, hi=hi, c=z_hi)
        )

    def tile_wait(o, c):
        remote(mine, place((z_lo - o + Z_LO) % Z_LO, c), z_s.at[0, 0], z_r.at[o, c], partner).wait_recv()

    high = jnp.logical_not(low)

    @pl.when(high)
    def _():
        for o in range(Z_LO):
            tile_copy(o, 0).start()

    for o in range(Z_LO - 1, 0, -1):
        tile_copy(o, z_hi).start()

    @pl.when(jnp.logical_not(native))
    def _():
        tile_copy(0, z_hi).start()

    def go(device):
        pl.semaphore_signal(go_sem, inc=1, device_id=device, device_id_type=MESH)

    @pl.when(jnp.logical_and(high, jnp.logical_not(native)))
    def _():
        go(at(hi=0))

    loads[3].wait()
    loads[4].wait()
    swaps = [
        remote(owner.at[core], owner.at[core], sw_s.at[0], sw_r.at[0], partner),
        remote(doc.at[core], doc.at[core], sw_s.at[1], sw_r.at[1], partner),
        remote(rows_hbm, rows.at[core], sw_s.at[2], sw_r.at[2], partner),
    ]
    for copy in swaps:
        copy.start()

    swaps[0].wait()
    swaps[1].wait()
    id_table = jnp.zeros((owners, 128), F32)
    for side in range(2):
        owner_row = owner[side]
        table = iota((owners, count), 0) == owner_row
        earlier = dot(table.astype(BF16), before[...], NN)
        rank = jnp.sum(jnp.where(table, earlier, 0.0), axis=0, keepdims=True).astype(jnp.int32)
        slot = owner_row * cap + rank
        pick[side] = (iota((owners * cap, count), 0) == slot).astype(BF16)
        doc_side = jnp.where(table, (doc[side] + 1).astype(F32), 0.0).astype(BF16)
        lane_side = (iota((128, count), 0) == side * cap + rank).astype(BF16)
        id_table = id_table + dot(doc_side, lane_side, NT)
    id_send[...] = id_table.reshape(id_send.shape)
    own_piece = gathered.at[y, x]
    over = remote(own_piece, own_piece, p_s, p_r, at(hi=1))
    by_piece = jnp.logical_and(high, jnp.logical_not(native))

    @pl.when(by_piece)
    def _():
        over.wait_recv()

    @pl.when(jnp.logical_not(by_piece))
    def _():
        @pl.when(jnp.logical_not(native))
        def _():
            tile_wait(0, 0)
            tile_wait(0, 1)

        @pl.when(native)
        def _():
            tile_wait(0, 1 - core)

        for o in range(1, Z_LO):
            for c in range(2):
                tile_wait(o, c)
        left = [tiles[i].astype(F32).reshape(Z_LO // 2 * 8, 128).astype(BF16) for i in range(4)]
        mixed = dot(jnp.concatenate(left, axis=1), turn[...], NN)
        for p in range(Z_LO // 2):
            part = [mixed[8 * p:8 * p + 8, 128 * j:128 * j + 128] for j in range(4)]
            for half in range(2):
                both = jnp.concatenate(part[2 * half:2 * half + 2], axis=0)
                gathered[y, x, half, :, 128 * p:128 * p + 128] = both.astype(BF16)

    def piece(dx, dy, half):
        return gathered.at[(y - dy + Y) % Y, (x - dx + X) % X, half]

    sizes = ((X, Y), (Y, X))

    def first_copy(half, j):
        device = at(dx=j) if half == 0 else at(dy=j)
        own = piece(0, 0, half)
        return remote(own, own, f_s.at[half, j], f_r.at[half, j], device)

    def second_copy(half, i, j):
        part = piece(i, 0, half) if half == 0 else piece(0, i, half)
        device = at(dy=j) if half == 0 else at(dx=j)
        return remote(part, part, g_s.at[half, i, j], g_r.at[half, i, j], device)

    copies = []

    def begin(copy):
        copy.start()
        copies.append(copy)

    for j in (2, 1, 3):
        for half in range(2):
            if j < sizes[half][0]:
                begin(first_copy(half, j))
    for i in (0, 1, 3, 2):
        for half in range(2):
            if i >= sizes[half][0]:
                continue
            if i:
                first_copy(half, i).wait_recv()
            for j in (2, 1, 3):
                if j < sizes[half][1]:
                    begin(second_copy(half, i, j))
        if i == 0:
            @pl.when(jnp.logical_and(low, native))
            def _():
                pl.semaphore_wait(go_sem, 1)
                over.start()

    def target(t):
        dz, dx, e = t // (2 * X), t // 2 % X, t % 2
        return ((x + dx) % X * Z_LO + dz) * 2 + e

    def id_copy(other):
        return remote(id_send.at[other], id_got.at[chip], i_s.at[other], i_r.at[chip], {"docs": other, "blk": b})

    def id_wait(i):
        remote(id_send.at[0], id_got.at[i], i_s.at[0], i_r.at[i], partner).wait_recv()

    def score_copy(other):
        return remote(
            send.at[other], got.at[core, chip], a_s.at[other], a_r.at[core, chip], {"docs": other, "blk": b}
        )

    def score_wait(c, i):
        remote(send.at[0], got.at[c, i], a_s.at[0], a_r.at[c, i], partner).wait_recv()

    def others(fn):
        def step(t, carry):
            other = target(t)

            @pl.when(other != d)
            def _():
                fn(other)

            return carry

        lax.fori_loop(0, owners, step, 0)

    def loop(start, stop, fn):
        lax.fori_loop(start, stop, lambda i, c: (fn(i), c)[1], 0)

    own_ids = pltpu.make_async_copy(id_send.at[d], id_got.at[chip], loc_sem.at[6])

    @pl.when(native)
    def _():
        others(lambda other: id_copy(other).start())
        own_ids.start()

    loads[2].wait()
    swaps[2].wait()
    for half in range(2):
        for i in range(sizes[half][0]):
            for j in range(1, sizes[half][1]):
                second_copy(half, i, j).wait_recv()

    span = gathered.shape[4]
    packed = []
    for side in range(2):
        part = None
        for i in range(X):
            term = dot(rows[side, :, i * span:(i + 1) * span], gathered[:, i].reshape(-1, span), NT)
            part = term if part is None else part + term
        packed.append(dot(pick[side], part.astype(BF16), NN).reshape(owners, cap, -1))
    send[...] = jnp.concatenate(packed, axis=1).astype(BF16)

    @pl.when(native)
    def _():
        own_ids.wait()

    @pl.when(jnp.logical_not(native))
    def _():
        id_wait(chip)

    others(lambda other: score_copy(other).start())
    own_scores = pltpu.make_async_copy(send.at[d], got.at[core, chip], loc_sem.at[7])
    own_scores.start()

    loop(1, chips, lambda i: id_wait((chip + i) % chips))
    per = chips * 2 * cap
    spread = (iota((per, chips), 0) // (2 * cap) == iota((per, chips), 1)).astype(BF16)
    ids = dot(spread, id_got[...].reshape(chips, 128).astype(BF16), NN)
    keep = iota(ids.shape, 1) == iota(ids.shape, 0) % (2 * cap)
    column = jnp.sum(jnp.where(keep, ids, 0.0), axis=1, keepdims=True).astype(jnp.int32) - 1
    member = (column == iota((per, weight.shape[1]), 1)).astype(BF16)
    loads[5].wait()

    own_scores.wait()
    for first in range(2):
        c = z_hi if first == 0 else 1 - z_hi

        @pl.when(c != core)
        def _():
            score_wait(c, chip)

        loop(1, chips, lambda i: score_wait(c, (chip + i) % chips))
        total = dot(got[c].reshape(per, -1), member, TN) * weight[...]
        size = total.shape[0] // Y
        for k in range(Y):
            for nh in range(2):
                out_ref[k, c, pl.ds(nh, size, stride=2), :] = total[k * size:(k + 1) * size, nh * 128:nh * 128 + 128]

    @pl.when(high)
    def _():
        for o in range(Z_LO):
            tile_copy(o, 0).wait_send()

    for o in range(1, Z_LO):
        tile_copy(o, z_hi).wait_send()

    @pl.when(jnp.logical_not(native))
    def _():
        tile_copy(0, z_hi).wait_send()

    @pl.when(native)
    def _():
        others(lambda other: id_copy(other).wait_send())

    @pl.when(jnp.logical_and(low, native))
    def _():
        over.wait_send()

    for copy in copies:
        copy.wait_send()
    others(lambda other: score_copy(other).wait_send())


def shards(group_rows, group_owner, group_doc, doc_weight, queries, precond):
    rows = group_rows[0]
    count, width = rows.shape
    docs, blks = lax.axis_size("docs"), lax.axis_size("blk")
    chips = X * Z_LO
    cap = 2 * count // docs
    own_q, part = queries.shape[0], precond.shape[1]
    doc_count = doc_weight.shape[1]
    dma = pltpu.SemaphoreType.DMA
    any_spec = pl.BlockSpec(memory_space=pl.ANY)
    vmem = pl.BlockSpec(memory_space=pltpu.VMEM)
    nx = max(X, Y)
    total = pl.pallas_call(
        kernel,
        out_shape=jax.ShapeDtypeStruct((Y, 2, 2 * own_q, doc_count // 2), F32),
        in_specs=[any_spec] * 6,
        out_specs=vmem,
        scratch_shapes=[
            pltpu.VMEM((2, count, width), BF16),
            pltpu.VMEM((2, 1, count), jnp.int32),
            pltpu.VMEM((2, 1, count), jnp.int32),
            pltpu.VMEM((1, doc_count), F32),
            pltpu.VMEM(queries.shape, BF16),
            pltpu.VMEM((part, width), BF16),
            pltpu.VMEM((8, 128), BF16),
            pltpu.VMEM((4, Z_LO // 2, 8, 128), BF16),
            pltpu.VMEM((Y, X, 2, own_q // 2, width // X), BF16),
            pltpu.VMEM((2, docs * cap, count), BF16),
            pltpu.VMEM((docs, 1, 128), F32),
            pltpu.VMEM((chips, 1, 128), F32),
            pltpu.VMEM((docs, 2 * cap, Y * own_q), BF16),
            pltpu.VMEM((2, chips, 2 * cap, Y * own_q), BF16),
            pltpu.VMEM((count, count), BF16),
            pltpu.VMEM((512, 512), BF16),
            dma((8,)), pltpu.SemaphoreType.REGULAR, dma((3,)), dma((3,)),
            dma((2, Z_LO)), dma((Z_LO, 2)), dma((2, nx)), dma((2, nx)), dma((2, nx, nx)), dma((2, nx, nx)), dma, dma,
            dma((docs,)), dma((chips,)), dma((docs,)), dma((2, chips)),
        ],
        compiler_params=pltpu.CompilerParams(collective_id=0, has_side_effects=True),
    )(rows, group_owner.reshape(1, count), group_doc, doc_weight, queries, precond.T)
    return total.reshape(blks * own_q, 1, doc_count)


def solution(mesh):
    return jax.shard_map(
        shards,
        mesh=mesh,
        in_specs=(
            P("blk", "docs", None),
            P("blk", "docs", None),
            P("blk", "docs"),
            P("blk", "docs"),
            P("blk", None),
            P(None, "docs"),
        ),
        out_specs=P(None, "blk", "docs"),
        check_vma=False,
    )
```

```python
import jax
import jax.numpy as jnp
from jax import lax
from jax.experimental import pallas as pl
from jax.experimental.pallas import tpu as pltpu
from jax.sharding import PartitionSpec as P

X, Y, Z_LO, Z_HI = 4, 4, 8, 2
REACH = 4
MESH = pl.DeviceIdType.MESH
NN = (((1,), (0,)), ((), ()))
NT = (((1,), (1,)), ((), ()))
TN = (((0,), (0,)), ((), ()))
F32, BF16 = jnp.float32, jnp.bfloat16


def dot(a, b, dims):
    return lax.dot_general(a, b, dims, preferred_element_type=F32)


def iota(shape, axis):
    return lax.broadcasted_iota(jnp.int32, shape, axis)


def kernel(
    rows_hbm, owner_hbm, doc_hbm, weight_hbm, query_hbm, pre_hbm, out_ref,
    rows, owner, doc, weight, query, pre, mine, tiles, gathered, pick,
    id_send, id_got, send, got, before, turn,
    loc_sem, go_sem, sw_s, sw_r, z_s, z_r, r_s, f_s, f_r, g_s, g_r, p_s, p_r,
    i_s, i_r, a_s, a_r,
):
    chips = X * Z_LO
    count = rows.shape[1]
    owners = 2 * chips
    cap = 2 * count // owners
    d, b = lax.axis_index("docs"), lax.axis_index("blk")
    core, chip = d % 2, d // 2
    x, z_lo = chip // Z_LO, chip % Z_LO
    y, z_hi = b // Z_HI, b % Z_HI
    native = core == z_hi
    low = z_hi == 0

    def at(dx=0, dy=0, lo=None, hi=None, c=None):
        lo, hi, c = (z_lo if lo is None else lo), (z_hi if hi is None else hi), (core if c is None else c)
        return {"docs": ((x + dx) % X * Z_LO + lo) * 2 + c, "blk": (y + dy) % Y * Z_HI + hi}

    def remote(src, dst, s, r, device):
        return pltpu.make_async_remote_copy(
            src_ref=src, dst_ref=dst, send_sem=s, recv_sem=r, device_id=device, device_id_type=MESH
        )

    barrier = pltpu.get_barrier_semaphore()

    def greet(device):
        pl.semaphore_signal(barrier, inc=1, device_id=device, device_id_type=MESH)

    for j in range(1, X):
        greet(at(dx=j))
    for j in range(1, Y):
        greet(at(dy=j))
    partner = at(c=1 - core)

    def near(o):
        lo = (z_lo + o) % Z_LO
        gap = jnp.abs(lo - z_lo)
        return lo, jnp.logical_or(low, gap <= REACH)

    @pl.when(native)
    def _():
        greet(partner)
        for o in range(1, Z_LO):
            lo, close = near(o)

            @pl.when(close)
            def _():
                for c in range(2):
                    greet(at(lo=lo, c=c))

    @pl.when(jnp.logical_not(native))
    def _():
        greet(partner)

    @pl.when(jnp.logical_and(low, native))
    def _():
        greet(at(hi=1))

    @pl.when(jnp.logical_and(low, jnp.logical_not(native)))
    def _():
        for o in range(Z_LO):
            for c in range(2):
                greet(at(lo=(z_lo + o) % Z_LO, hi=1, c=c))

    loads = [
        pltpu.make_async_copy(src, dst, loc_sem.at[i])
        for i, (src, dst) in enumerate(
            [
                (query_hbm, query), (pre_hbm, pre), (rows_hbm, rows.at[core]),
                (owner_hbm, owner.at[core]), (doc_hbm, doc.at[core]), (weight_hbm, weight),
            ]
        )
    ]
    for copy in loads:
        copy.start()

    before[...] = (iota((count, count), 0) < iota((count, count), 1)).astype(BF16)
    n = 4 * 128
    row, col = iota((n, n), 0), iota((n, n), 1)
    placed = (row // 128 == col % 128 // 32) & (row % 128 // 32 == col // 128) & (row % 32 == col % 32)
    turn[...] = placed.astype(BF16)

    loads[0].wait()
    loads[1].wait()
    block = dot(query[...], jnp.concatenate([pre[...]] * 4, axis=0), NT)
    group = iota((8, 128), 1) // 32
    tile = jnp.zeros((8, 128), F32)
    for j in range(4):
        tile = jnp.where(group == j, block[8 * j:8 * j + 8], tile)
    tile = tile.astype(BF16)
    mine[...] = tile

    def place(lo, c):
        return tiles.at[lo % 2 * 2 + c, lo // 2]

    @pl.when(native)
    def _():
        tiles[z_lo % 2 * 2 + core, z_lo // 2] = tile

    few = 2 * X + 2 * Y - 2 - (X + Y) + Z_LO
    many = few + Z_LO
    beyond = jnp.maximum(0, jnp.maximum(Z_LO - 1 - REACH - z_lo, z_lo - REACH))
    pl.semaphore_wait(barrier, jnp.where(low, few, many - beyond + jnp.where(native, 0, 1)))

    def tile_copy(o, hi, c=None):
        return remote(
            mine, place(z_lo, core), z_s.at[hi, o], z_r.at[o, core], at(lo=(z_lo + o) % Z_LO, hi=hi, c=z_hi)
        )

    def tile_wait(o, c):
        remote(mine, place((z_lo - o + Z_LO) % Z_LO, c), z_s.at[0, 0], z_r.at[o, c], partner).wait_recv()

    high = jnp.logical_not(low)
    first_side = z_lo < Z_LO - REACH

    def passed(o):
        lo = (z_lo - o + Z_LO) % Z_LO
        on = jnp.where(first_side, lo < z_lo, jnp.logical_and(z_lo >= REACH, lo > z_lo))
        return jnp.logical_and(jnp.logical_and(high, native), on)

    def passing(fn):
        goal = jnp.where(first_side, z_lo + REACH, jnp.maximum(z_lo - REACH, 0))
        for o in range(1, Z_LO):
            lo = (z_lo - o + Z_LO) % Z_LO

            @pl.when(passed(o))
            def _():
                for c in range(2):
                    tile = place(lo, c)
                    away = (goal - lo + Z_LO) % Z_LO
                    fn(remote(tile, tile, r_s.at[o, c], z_r.at[away, c], at(lo=goal)), o, c)


    @pl.when(high)
    def _():
        for o in range(Z_LO):
            tile_copy(o, 0).start()

    for o in range(Z_LO - 1, 0, -1):
        @pl.when(near(o)[1])
        def _():
            tile_copy(o, z_hi).start()

    @pl.when(jnp.logical_not(native))
    def _():
        tile_copy(0, z_hi).start()

    def go(device):
        pl.semaphore_signal(go_sem, inc=1, device_id=device, device_id_type=MESH)

    @pl.when(jnp.logical_and(high, jnp.logical_not(native)))
    def _():
        go(at(hi=0))

    loads[3].wait()
    loads[4].wait()
    swaps = [
        remote(owner.at[core], owner.at[core], sw_s.at[0], sw_r.at[0], partner),
        remote(doc.at[core], doc.at[core], sw_s.at[1], sw_r.at[1], partner),
        remote(rows_hbm, rows.at[core], sw_s.at[2], sw_r.at[2], partner),
    ]
    for copy in swaps:
        copy.start()

    swaps[0].wait()
    swaps[1].wait()
    id_table = jnp.zeros((owners, 128), F32)
    for side in range(2):
        owner_row = owner[side]
        table = iota((owners, count), 0) == owner_row
        earlier = dot(table.astype(BF16), before[...], NN)
        rank = jnp.sum(jnp.where(table, earlier, 0.0), axis=0, keepdims=True).astype(jnp.int32)
        slot = (owner_row * 2 + side) * cap + rank
        pick[:, side * count:(side + 1) * count] = (iota((owners * 2 * cap, count), 0) == slot).astype(BF16)
        doc_side = jnp.where(table, (doc[side] + 1).astype(F32), 0.0).astype(BF16)
        lane_side = (iota((128, count), 0) == side * cap + rank).astype(BF16)
        id_table = id_table + dot(doc_side, lane_side, NT)
    id_send[...] = id_table.reshape(id_send.shape)
    own_piece = gathered.at[y, x]
    over = remote(own_piece, own_piece, p_s, p_r, at(hi=1))
    by_piece = jnp.logical_and(high, jnp.logical_not(native))

    @pl.when(by_piece)
    def _():
        over.wait_recv()

    @pl.when(jnp.logical_not(by_piece))
    def _():
        @pl.when(jnp.logical_not(native))
        def _():
            tile_wait(0, 0)
            tile_wait(0, 1)

        @pl.when(native)
        def _():
            tile_wait(0, 1 - core)

        @pl.when(jnp.logical_and(high, native))
        def _():
            def forward(copy, o, c):
                tile_wait(o, c)
                copy.start()

            passing(forward)

        for o in range(1, Z_LO):
            @pl.when(jnp.logical_not(passed(o)))
            def _():
                for c in range(2):
                    tile_wait(o, c)
        left = [tiles[i].astype(F32).reshape(Z_LO // 2 * 8, 128).astype(BF16) for i in range(4)]
        mixed = dot(jnp.concatenate(left, axis=1), turn[...], NN)
        for p in range(Z_LO // 2):
            part = [mixed[8 * p:8 * p + 8, 128 * j:128 * j + 128] for j in range(4)]
            for half in range(2):
                both = jnp.concatenate(part[2 * half:2 * half + 2], axis=0)
                gathered[y, x, half, :, 128 * p:128 * p + 128] = both.astype(BF16)

    def piece(dx, dy, half):
        return gathered.at[(y - dy + Y) % Y, (x - dx + X) % X, half]

    sizes = ((X, Y), (Y, X))

    def first_copy(half, j):
        device = at(dx=j) if half == 0 else at(dy=j)
        own = piece(0, 0, half)
        return remote(own, own, f_s.at[half, j], f_r.at[half, j], device)

    def second_copy(half, i, j):
        part = piece(i, 0, half) if half == 0 else piece(0, i, half)
        device = at(dy=j) if half == 0 else at(dx=j)
        return remote(part, part, g_s.at[half, i, j], g_r.at[half, i, j], device)

    copies = []

    def begin(copy):
        copy.start()
        copies.append(copy)

    for j in (2, 1, 3):
        for half in range(2):
            if j < sizes[half][0]:
                begin(first_copy(half, j))
    for i in (0, 1, 3, 2):
        for half in range(2):
            if i >= sizes[half][0]:
                continue
            if i:
                first_copy(half, i).wait_recv()
            for j in (2, 1, 3):
                if j < sizes[half][1]:
                    begin(second_copy(half, i, j))
        if i == 0:
            @pl.when(jnp.logical_and(low, native))
            def _():
                pl.semaphore_wait(go_sem, 1)
                over.start()

    def target(t):
        dz, dx, e = t // (2 * X), t // 2 % X, t % 2
        to = dz
        return ((x + dx) % X * Z_LO + to) * 2 + e

    def id_copy(other):
        return remote(id_send.at[other], id_got.at[chip], i_s.at[other], i_r.at[chip], {"docs": other, "blk": b})

    def id_wait(i):
        remote(id_send.at[0], id_got.at[i], i_s.at[0], i_r.at[i], partner).wait_recv()

    def score_copy(other):
        return remote(
            send.at[other], got.at[core, chip], a_s.at[other], a_r.at[core, chip], {"docs": other, "blk": b}
        )

    def score_wait(c, i):
        remote(send.at[0], got.at[c, i], a_s.at[0], a_r.at[c, i], partner).wait_recv()

    def others(fn):
        def step(t, carry):
            other = target(t)

            @pl.when(other != d)
            def _():
                fn(other)

            return carry

        lax.fori_loop(0, owners, step, 0)

    def loop(start, stop, fn):
        lax.fori_loop(start, stop, lambda i, c: (fn(i), c)[1], 0)

    own_ids = pltpu.make_async_copy(id_send.at[d], id_got.at[chip], loc_sem.at[6])

    @pl.when(native)
    def _():
        others(lambda other: id_copy(other).start())
        own_ids.start()

    loads[2].wait()
    swaps[2].wait()
    for half in range(2):
        for i in range(sizes[half][0]):
            for j in range(1, sizes[half][1]):
                second_copy(half, i, j).wait_recv()

    span = gathered.shape[4]
    full = jnp.concatenate([gathered[:, i].reshape(-1, span) for i in range(X)], axis=1)
    part = jnp.concatenate([dot(rows[side], full, NT).astype(BF16) for side in range(2)], axis=0)
    send[...] = dot(pick[...], part, NN).astype(BF16).reshape(send.shape)

    @pl.when(native)
    def _():
        own_ids.wait()

    @pl.when(jnp.logical_not(native))
    def _():
        id_wait(chip)

    others(lambda other: score_copy(other).start())
    own_scores = pltpu.make_async_copy(send.at[d], got.at[core, chip], loc_sem.at[7])
    own_scores.start()

    loop(1, chips, lambda i: id_wait((chip + i) % chips))
    per = chips * 2 * cap
    spread = (iota((per, chips), 0) // (2 * cap) == iota((per, chips), 1)).astype(BF16)
    ids = dot(spread, id_got[...].reshape(chips, 128).astype(BF16), NN)
    keep = iota(ids.shape, 1) == iota(ids.shape, 0) % (2 * cap)
    column = jnp.sum(jnp.where(keep, ids, 0.0), axis=1, keepdims=True).astype(jnp.int32) - 1
    member = (column == iota((per, weight.shape[1]), 1)).astype(BF16)
    loads[5].wait()

    own_scores.wait()
    for first in range(2):
        c = z_hi if first == 0 else 1 - z_hi

        @pl.when(c != core)
        def _():
            score_wait(c, chip)

        loop(1, chips, lambda i: score_wait(c, (chip + i) % chips))
        total = dot(got[c].reshape(per, -1), member, TN) * weight[...]
        size = total.shape[0] // Y
        for k in range(Y):
            for nh in range(2):
                out_ref[k, c, pl.ds(nh, size, stride=2), :] = total[k * size:(k + 1) * size, nh * 128:nh * 128 + 128]

    @pl.when(high)
    def _():
        for o in range(Z_LO):
            tile_copy(o, 0).wait_send()

    for o in range(1, Z_LO):
        @pl.when(near(o)[1])
        def _():
            tile_copy(o, z_hi).wait_send()

    @pl.when(jnp.logical_and(high, native))
    def _():
        passing(lambda copy, o, c: copy.wait_send())

    @pl.when(jnp.logical_not(native))
    def _():
        tile_copy(0, z_hi).wait_send()

    @pl.when(native)
    def _():
        others(lambda other: id_copy(other).wait_send())

    @pl.when(jnp.logical_and(low, native))
    def _():
        over.wait_send()

    for copy in copies:
        copy.wait_send()
    others(lambda other: score_copy(other).wait_send())


def shards(group_rows, group_owner, group_doc, doc_weight, queries, precond):
    rows = group_rows[0]
    count, width = rows.shape
    docs, blks = lax.axis_size("docs"), lax.axis_size("blk")
    chips = X * Z_LO
    cap = 2 * count // docs
    own_q, part = queries.shape[0], precond.shape[1]
    doc_count = doc_weight.shape[1]
    dma = pltpu.SemaphoreType.DMA
    any_spec = pl.BlockSpec(memory_space=pl.ANY)
    vmem = pl.BlockSpec(memory_space=pltpu.VMEM)
    nx = max(X, Y)
    total = pl.pallas_call(
        kernel,
        out_shape=pltpu.VMEM((Y, 2, 2 * own_q, doc_count // 2), F32),
        in_specs=[any_spec] * 6,
        out_specs=vmem,
        scratch_shapes=[
            pltpu.VMEM((2, count, width), BF16),
            pltpu.VMEM((2, 1, count), jnp.int32),
            pltpu.VMEM((2, 1, count), jnp.int32),
            pltpu.VMEM((1, doc_count), F32),
            pltpu.VMEM(queries.shape, BF16),
            pltpu.VMEM((part, width), BF16),
            pltpu.VMEM((8, 128), BF16),
            pltpu.VMEM((4, Z_LO // 2, 8, 128), BF16),
            pltpu.VMEM((Y, X, 2, own_q // 2, width // X), BF16),
            pltpu.VMEM((docs * 2 * cap, 2 * count), BF16),
            pltpu.VMEM((docs, 1, 128), F32),
            pltpu.VMEM((chips, 1, 128), F32),
            pltpu.VMEM((docs, 2 * cap, Y * own_q), BF16),
            pltpu.VMEM((2, chips, 2 * cap, Y * own_q), BF16),
            pltpu.VMEM((count, count), BF16),
            pltpu.VMEM((512, 512), BF16),
            dma((8,)), pltpu.SemaphoreType.REGULAR, dma((3,)), dma((3,)),
            dma((2, Z_LO)), dma((Z_LO, 2)), dma((Z_LO, 2)), dma((2, nx)), dma((2, nx)), dma((2, nx, nx)), dma((2, nx, nx)), dma, dma,
            dma((docs,)), dma((chips,)), dma((docs,)), dma((2, chips)),
        ],
        compiler_params=pltpu.CompilerParams(collective_id=0, has_side_effects=True),
    )(rows, group_owner.reshape(1, count), group_doc, doc_weight, queries, precond.T)
    return total.reshape(blks * own_q, 1, doc_count)


def solution(mesh):
    return jax.shard_map(
        shards,
        mesh=mesh,
        in_specs=(
            P("blk", "docs", None),
            P("blk", "docs", None),
            P("blk", "docs"),
            P("blk", "docs"),
            P("blk", None),
            P(None, "docs"),
        ),
        out_specs=P(None, "blk", "docs"),
        check_vma=False,
    )
```

```python
import jax
import jax.numpy as jnp
from jax import lax
from jax.experimental import pallas as pl
from jax.experimental.pallas import tpu as pltpu
from jax.sharding import PartitionSpec as P

X, Y, Z_LO, Z_HI = 4, 4, 8, 2
REACH = 4
MESH = pl.DeviceIdType.MESH
NN = (((1,), (0,)), ((), ()))
NT = (((1,), (1,)), ((), ()))
TN = (((0,), (0,)), ((), ()))
F32, BF16 = jnp.float32, jnp.bfloat16


def dot(a, b, dims):
    return lax.dot_general(a, b, dims, preferred_element_type=F32)


def iota(shape, axis):
    return lax.broadcasted_iota(jnp.int32, shape, axis)


def kernel(
    rows_hbm, owner_hbm, doc_hbm, weight_hbm, query_hbm, pre_hbm, out_ref,
    rows, owner, doc, weight, query, pre, mine, tiles, gathered, pick,
    id_send, id_got, send, got, before, turn,
    loc_sem, go_sem, sw_s, sw_r, z_s, z_r, r_s, f_s, f_r, g_s, g_r, p_s, p_r,
    i_s, i_r, a_s, a_r,
):
    chips = X * Z_LO
    count = rows.shape[1]
    owners = 2 * chips
    cap = 2 * count // owners
    d, b = lax.axis_index("docs"), lax.axis_index("blk")
    core, chip = d % 2, d // 2
    x, z_lo = chip // Z_LO, chip % Z_LO
    y, z_hi = b // Z_HI, b % Z_HI
    native = core == z_hi
    low = z_hi == 0

    def at(dx=0, dy=0, lo=None, hi=None, c=None):
        lo, hi, c = (z_lo if lo is None else lo), (z_hi if hi is None else hi), (core if c is None else c)
        return {"docs": ((x + dx) % X * Z_LO + lo) * 2 + c, "blk": (y + dy) % Y * Z_HI + hi}

    def remote(src, dst, s, r, device):
        return pltpu.make_async_remote_copy(
            src_ref=src, dst_ref=dst, send_sem=s, recv_sem=r, device_id=device, device_id_type=MESH
        )

    barrier = pltpu.get_barrier_semaphore()

    def greet(device):
        pl.semaphore_signal(barrier, inc=1, device_id=device, device_id_type=MESH)

    for j in range(1, X):
        greet(at(dx=j))
    for j in range(1, Y):
        greet(at(dy=j))
    partner = at(c=1 - core)

    def near(o):
        lo = (z_lo + o) % Z_LO
        return lo, jnp.abs(lo - z_lo) <= REACH

    @pl.when(native)
    def _():
        greet(partner)
        for o in range(1, Z_LO):
            lo, close = near(o)

            @pl.when(close)
            def _():
                for c in range(2):
                    greet(at(lo=lo, c=c))

    @pl.when(jnp.logical_not(native))
    def _():
        greet(partner)

    @pl.when(jnp.logical_and(low, native))
    def _():
        greet(at(hi=1))

    @pl.when(jnp.logical_and(low, jnp.logical_not(native)))
    def _():
        for o in range(Z_LO):
            for c in range(2):
                greet(at(lo=(z_lo + o) % Z_LO, hi=1, c=c))

    loads = [
        pltpu.make_async_copy(src, dst, loc_sem.at[i])
        for i, (src, dst) in enumerate(
            [
                (query_hbm, query), (pre_hbm, pre), (rows_hbm, rows.at[core]),
                (owner_hbm, owner.at[core]), (doc_hbm, doc.at[core]), (weight_hbm, weight),
            ]
        )
    ]
    for copy in loads:
        copy.start()

    before[...] = (iota((count, count), 0) < iota((count, count), 1)).astype(BF16)
    n = 4 * 128
    row, col = iota((n, n), 0), iota((n, n), 1)
    placed = (row // 128 == col % 128 // 32) & (row % 128 // 32 == col // 128) & (row % 32 == col % 32)
    turn[...] = placed.astype(BF16)

    loads[0].wait()
    loads[1].wait()
    block = dot(query[...], jnp.concatenate([pre[...]] * 4, axis=0), NT)
    group = iota((8, 128), 1) // 32
    tile = jnp.zeros((8, 128), F32)
    for j in range(4):
        tile = jnp.where(group == j, block[8 * j:8 * j + 8], tile)
    tile = tile.astype(BF16)
    mine[...] = tile

    def place(lo, c):
        return tiles.at[lo % 2 * 2 + c, lo // 2]

    @pl.when(native)
    def _():
        tiles[z_lo % 2 * 2 + core, z_lo // 2] = tile

    few = 2 * X + 2 * Y - 2 - (X + Y) + Z_LO
    many = few + Z_LO
    beyond = jnp.maximum(0, jnp.maximum(Z_LO - 1 - REACH - z_lo, z_lo - REACH))
    pl.semaphore_wait(barrier, jnp.where(low, few, many + jnp.where(native, 0, 1)) - beyond)

    def tile_copy(o, hi, c=None):
        return remote(
            mine, place(z_lo, core), z_s.at[hi, o], z_r.at[o, core], at(lo=(z_lo + o) % Z_LO, hi=hi, c=z_hi)
        )

    def tile_wait(o, c):
        remote(mine, place((z_lo - o + Z_LO) % Z_LO, c), z_s.at[0, 0], z_r.at[o, c], partner).wait_recv()

    high = jnp.logical_not(low)
    first_side = z_lo < Z_LO - REACH

    def passed(o):
        lo = (z_lo - o + Z_LO) % Z_LO
        on = jnp.where(first_side, lo < z_lo, jnp.logical_and(z_lo >= REACH, lo > z_lo))
        return jnp.logical_and(native, on)

    def passing(fn):
        goal = jnp.where(first_side, z_lo + REACH, jnp.maximum(z_lo - REACH, 0))
        for o in range(1, Z_LO):
            lo = (z_lo - o + Z_LO) % Z_LO

            @pl.when(passed(o))
            def _():
                for c in range(2):
                    tile = place(lo, c)
                    away = (goal - lo + Z_LO) % Z_LO
                    fn(remote(tile, tile, r_s.at[o, c], z_r.at[away, c], at(lo=goal)), o, c)


    @pl.when(high)
    def _():
        for o in range(Z_LO):
            tile_copy(o, 0).start()

    for o in range(Z_LO - 1, 0, -1):
        @pl.when(near(o)[1])
        def _():
            tile_copy(o, z_hi).start()

    @pl.when(jnp.logical_not(native))
    def _():
        tile_copy(0, z_hi).start()

    def go(device):
        pl.semaphore_signal(go_sem, inc=1, device_id=device, device_id_type=MESH)

    @pl.when(jnp.logical_and(high, jnp.logical_not(native)))
    def _():
        go(at(hi=0))

    loads[3].wait()
    loads[4].wait()
    swaps = [
        remote(owner.at[core], owner.at[core], sw_s.at[0], sw_r.at[0], partner),
        remote(doc.at[core], doc.at[core], sw_s.at[1], sw_r.at[1], partner),
        remote(rows_hbm, rows.at[core], sw_s.at[2], sw_r.at[2], partner),
    ]
    for copy in swaps:
        copy.start()

    swaps[0].wait()
    swaps[1].wait()
    id_table = jnp.zeros((owners, 128), F32)
    for side in range(2):
        owner_row = owner[side]
        table = iota((owners, count), 0) == owner_row
        earlier = dot(table.astype(BF16), before[...], NN)
        rank = jnp.sum(jnp.where(table, earlier, 0.0), axis=0, keepdims=True).astype(jnp.int32)
        slot = (owner_row * 2 + side) * cap + rank
        pick[:, side * count:(side + 1) * count] = (iota((owners * 2 * cap, count), 0) == slot).astype(BF16)
        doc_side = jnp.where(table, (doc[side] + 1).astype(F32), 0.0).astype(BF16)
        lane_side = (iota((128, count), 0) == side * cap + rank).astype(BF16)
        id_table = id_table + dot(doc_side, lane_side, NT)
    id_send[...] = id_table.reshape(id_send.shape)
    own_piece = gathered.at[y, x]
    over = remote(own_piece, own_piece, p_s, p_r, at(hi=1))
    by_piece = jnp.logical_and(high, jnp.logical_not(native))

    @pl.when(by_piece)
    def _():
        over.wait_recv()

    @pl.when(jnp.logical_not(by_piece))
    def _():
        @pl.when(jnp.logical_not(native))
        def _():
            tile_wait(0, 0)
            tile_wait(0, 1)

        @pl.when(native)
        def _():
            tile_wait(0, 1 - core)

        @pl.when(native)
        def _():
            def forward(copy, o, c):
                tile_wait(o, c)
                copy.start()

            passing(forward)

        for o in range(1, Z_LO):
            @pl.when(jnp.logical_not(passed(o)))
            def _():
                for c in range(2):
                    tile_wait(o, c)
        left = [tiles[i].astype(F32).reshape(Z_LO // 2 * 8, 128).astype(BF16) for i in range(4)]
        mixed = dot(jnp.concatenate(left, axis=1), turn[...], NN)
        for p in range(Z_LO // 2):
            part = [mixed[8 * p:8 * p + 8, 128 * j:128 * j + 128] for j in range(4)]
            for half in range(2):
                both = jnp.concatenate(part[2 * half:2 * half + 2], axis=0)
                gathered[y, x, half, :, 128 * p:128 * p + 128] = both.astype(BF16)

    def piece(dx, dy, half):
        return gathered.at[(y - dy + Y) % Y, (x - dx + X) % X, half]

    sizes = ((X, Y), (Y, X))

    def first_copy(half, j):
        device = at(dx=j) if half == 0 else at(dy=j)
        own = piece(0, 0, half)
        return remote(own, own, f_s.at[half, j], f_r.at[half, j], device)

    def second_copy(half, i, j):
        part = piece(i, 0, half) if half == 0 else piece(0, i, half)
        device = at(dy=j) if half == 0 else at(dx=j)
        return remote(part, part, g_s.at[half, i, j], g_r.at[half, i, j], device)

    copies = []

    def begin(copy):
        copy.start()
        copies.append(copy)

    for j in (2, 1, 3):
        for half in range(2):
            if j < sizes[half][0]:
                begin(first_copy(half, j))
    for i in (0, 1, 3, 2):
        for half in range(2):
            if i >= sizes[half][0]:
                continue
            if i:
                first_copy(half, i).wait_recv()
            for j in (2, 1, 3):
                if j < sizes[half][1]:
                    begin(second_copy(half, i, j))
        if i == 0:
            @pl.when(jnp.logical_and(low, native))
            def _():
                pl.semaphore_wait(go_sem, 1)
                over.start()

    def target(t):
        dz, dx, e = t // (2 * X), t // 2 % X, t % 2
        to = dz
        return ((x + dx) % X * Z_LO + to) * 2 + e

    def id_copy(other):
        return remote(id_send.at[other], id_got.at[chip], i_s, i_r.at[0], {"docs": other, "blk": b})

    mate = d + 1 - 2 * core
    mate_ids = remote(id_send.at[mate], id_got.at[chip], i_s, i_r.at[1], partner)

    def score_copy(other):
        return remote(
            send.at[other], got.at[core, chip], a_s, a_r.at[core], {"docs": other, "blk": b}
        )

    def settle(ref, sem):
        pltpu.make_async_copy(ref, ref, sem).wait()

    def others(fn):
        def step(t, carry):
            other = target(t)

            @pl.when(other // 2 != chip)
            def _():
                fn(other)

            return carry

        lax.fori_loop(0, owners, step, 0)

    own_ids = pltpu.make_async_copy(id_send.at[d], id_got.at[chip], loc_sem.at[6])

    @pl.when(native)
    def _():
        others(lambda other: id_copy(other).start())
        mate_ids.start()
        own_ids.start()

    loads[2].wait()
    swaps[2].wait()
    span = gathered.shape[4]
    sums = [None, None]
    for i in (0, 1, 3, 2):
        if i >= X:
            continue
        for j in range(1, Y):
            second_copy(0, i, j).wait_recv()
        for j in range(Y if i else 0):
            second_copy(1, j, i).wait_recv()
        at_x = (x - i + X) % X
        right = gathered[:, at_x].reshape(-1, span)
        for side in range(2):
            term = dot(rows[side, :, pl.ds(pl.multiple_of(at_x * span, span), span)], right, NT)
            sums[side] = term if sums[side] is None else sums[side] + term
    part = jnp.concatenate([total.astype(BF16) for total in sums], axis=0)
    send[...] = dot(pick[...], part, NN).astype(BF16).reshape(send.shape)

    @pl.when(native)
    def _():
        own_ids.wait()

    @pl.when(jnp.logical_not(native))
    def _():
        mate_ids.wait_recv()

    others(lambda other: score_copy(other).start())
    score_copy(mate).start()
    own_scores = pltpu.make_async_copy(send.at[d], got.at[core, chip], a_r.at[core])
    own_scores.start()

    settle(id_got.at[pl.ds(0, chips - 1)], i_r.at[0])
    per = chips * 2 * cap
    spread = (iota((per, chips), 0) // (2 * cap) == iota((per, chips), 1)).astype(BF16)
    ids = dot(spread, id_got[...].reshape(chips, 128).astype(BF16), NN)
    keep = iota(ids.shape, 1) == iota(ids.shape, 0) % (2 * cap)
    column = jnp.sum(jnp.where(keep, ids, 0.0), axis=1, keepdims=True).astype(jnp.int32) - 1
    member = (column == iota((per, weight.shape[1]), 1)).astype(BF16)
    loads[5].wait()

    @pl.when(high)
    def _():
        for o in range(Z_LO):
            tile_copy(o, 0).wait_send()

    for o in range(1, Z_LO):
        @pl.when(near(o)[1])
        def _():
            tile_copy(o, z_hi).wait_send()

    @pl.when(native)
    def _():
        passing(lambda copy, o, c: copy.wait_send())

    @pl.when(jnp.logical_not(native))
    def _():
        tile_copy(0, z_hi).wait_send()

    @pl.when(native)
    def _():
        settle(id_send.at[pl.ds(0, owners - 1)], i_s)

    @pl.when(jnp.logical_and(low, native))
    def _():
        over.wait_send()

    for copy in copies:
        copy.wait_send()
    for first in range(2):
        c = z_hi if first == 0 else 1 - z_hi
        if first:
            settle(send.at[pl.ds(0, owners - 1)], a_s)
        settle(got.at[c], a_r.at[c])
        total = dot(got[c].reshape(per, -1), member, TN) * weight[...]
        size = total.shape[0] // Y
        for k in range(Y):
            for nh in range(2):
                out_ref[k, c, pl.ds(nh, size, stride=2), :] = total[k * size:(k + 1) * size, nh * 128:nh * 128 + 128]


def shards(group_rows, group_owner, group_doc, doc_weight, queries, precond):
    rows = group_rows[0]
    count, width = rows.shape
    docs, blks = lax.axis_size("docs"), lax.axis_size("blk")
    chips = X * Z_LO
    cap = 2 * count // docs
    own_q, part = queries.shape[0], precond.shape[1]
    doc_count = doc_weight.shape[1]
    dma = pltpu.SemaphoreType.DMA
    any_spec = pl.BlockSpec(memory_space=pl.ANY)
    vmem = pl.BlockSpec(memory_space=pltpu.VMEM)
    nx = max(X, Y)
    total = pl.pallas_call(
        kernel,
        out_shape=pltpu.VMEM((Y, 2, 2 * own_q, doc_count // 2), F32),
        in_specs=[any_spec] * 6,
        out_specs=vmem,
        scratch_shapes=[
            pltpu.VMEM((2, count, width), BF16),
            pltpu.VMEM((2, 1, count), jnp.int32),
            pltpu.VMEM((2, 1, count), jnp.int32),
            pltpu.VMEM((1, doc_count), F32),
            pltpu.VMEM(queries.shape, BF16),
            pltpu.VMEM((part, width), BF16),
            pltpu.VMEM((8, 128), BF16),
            pltpu.VMEM((4, Z_LO // 2, 8, 128), BF16),
            pltpu.VMEM((Y, X, 2, own_q // 2, width // X), BF16),
            pltpu.VMEM((docs * 2 * cap, 2 * count), BF16),
            pltpu.VMEM((docs, 1, 128), F32),
            pltpu.VMEM((chips, 1, 128), F32),
            pltpu.VMEM((docs, 2 * cap, Y * own_q), BF16),
            pltpu.VMEM((2, chips, 2 * cap, Y * own_q), BF16),
            pltpu.VMEM((count, count), BF16),
            pltpu.VMEM((512, 512), BF16),
            dma((7,)), pltpu.SemaphoreType.REGULAR, dma((3,)), dma((3,)),
            dma((2, Z_LO)), dma((Z_LO, 2)), dma((Z_LO, 2)), dma((2, nx)), dma((2, nx)), dma((2, nx, nx)), dma((2, nx, nx)), dma, dma,
            dma, dma((2,)), dma, dma((2,)),
        ],
        compiler_params=pltpu.CompilerParams(collective_id=0, has_side_effects=True),
    )(rows, group_owner.reshape(1, count), group_doc, doc_weight, queries, precond.T)
    return total.reshape(blks * own_q, 1, doc_count)


def solution(mesh):
    return jax.shard_map(
        shards,
        mesh=mesh,
        in_specs=(
            P("blk", "docs", None),
            P("blk", "docs", None),
            P("blk", "docs"),
            P("blk", "docs"),
            P("blk", None),
            P(None, "docs"),
        ),
        out_specs=P(None, "blk", "docs"),
        check_vma=False,
    )
```

```python
import jax
import jax.numpy as jnp
from jax import lax
from jax.experimental import pallas as pl
from jax.experimental.pallas import tpu as pltpu
from jax.sharding import PartitionSpec as P

X, Y, Z_LO, Z_HI = 4, 4, 8, 2
REACH = 4
MESH = pl.DeviceIdType.MESH
NN = (((1,), (0,)), ((), ()))
NT = (((1,), (1,)), ((), ()))
TN = (((0,), (0,)), ((), ()))
F32, BF16 = jnp.float32, jnp.bfloat16


def dot(a, b, dims):
    return lax.dot_general(a, b, dims, preferred_element_type=F32)


def iota(shape, axis):
    return lax.broadcasted_iota(jnp.int32, shape, axis)


def kernel(
    rows_hbm, owner_hbm, doc_hbm, weight_hbm, query_hbm, pre_hbm, out_ref,
    rows, owner, doc, weight, query, pre, mine, tiles, gathered, pick,
    id_send, id_got, send, got, before, turn,
    loc_sem, go_sem, sw_s, sw_r, z_s, z_r, r_s, f_s, f_r, g_s, g_r, p_s, p_r,
    i_s, i_r, a_s, a_r,
):
    chips = X * Z_LO
    count = rows.shape[1]
    owners = 2 * chips
    cap = 2 * count // owners
    d, b = lax.axis_index("docs"), lax.axis_index("blk")
    core, chip = d % 2, d // 2
    x, z_lo = chip // Z_LO, chip % Z_LO
    y, z_hi = b // Z_HI, b % Z_HI
    native = core == z_hi
    low = z_hi == 0

    def at(dx=0, dy=0, lo=None, hi=None, c=None):
        lo, hi, c = (z_lo if lo is None else lo), (z_hi if hi is None else hi), (core if c is None else c)
        return {"docs": ((x + dx) % X * Z_LO + lo) * 2 + c, "blk": (y + dy) % Y * Z_HI + hi}

    def remote(src, dst, s, r, device):
        return pltpu.make_async_remote_copy(
            src_ref=src, dst_ref=dst, send_sem=s, recv_sem=r, device_id=device, device_id_type=MESH
        )

    loads = [
        pltpu.make_async_copy(src, dst, loc_sem.at[i])
        for i, (src, dst) in enumerate(
            [
                (query_hbm, query), (pre_hbm, pre), (rows_hbm, rows.at[core]),
                (owner_hbm, owner.at[core]), (doc_hbm, doc.at[core]), (weight_hbm, weight),
            ]
        )
    ]
    for copy in loads:
        copy.start()

    barrier = pltpu.get_barrier_semaphore()

    def greet(device):
        pl.semaphore_signal(barrier, inc=1, device_id=device, device_id_type=MESH)

    partner = at(c=1 - core)

    def near(o):
        lo = (z_lo + o) % Z_LO
        return lo, jnp.abs(lo - z_lo) <= REACH

    @pl.when(native)
    def _():
        for o in range(1, Z_LO):
            lo, close = near(o)

            @pl.when(close)
            def _():
                for c in range(2):
                    greet(at(lo=lo, c=c))

        greet(partner)

    @pl.when(jnp.logical_not(native))
    def _():
        greet(partner)

    @pl.when(jnp.logical_and(low, native))
    def _():
        greet(at(hi=1))

    @pl.when(jnp.logical_and(low, jnp.logical_not(native)))
    def _():
        for o in range(Z_LO):
            for c in range(2):
                greet(at(lo=(z_lo + o) % Z_LO, hi=1, c=c))

    for j in range(1, X):
        greet(at(dx=j))
    for j in range(1, Y):
        greet(at(dy=j))

    before[...] = (iota((count, count), 0) < iota((count, count), 1)).astype(BF16)
    n = 4 * 128
    row, col = iota((n, n), 0), iota((n, n), 1)
    placed = (row // 128 == col % 128 // 32) & (row % 128 // 32 == col // 128) & (row % 32 == col % 32)
    turn[...] = placed.astype(BF16)

    loads[0].wait()
    loads[1].wait()
    block = dot(query[...], jnp.concatenate([pre[...]] * 4, axis=0), NT)
    group = iota((8, 128), 1) // 32
    tile = jnp.zeros((8, 128), F32)
    for j in range(4):
        tile = jnp.where(group == j, block[8 * j:8 * j + 8], tile)
    tile = tile.astype(BF16)
    mine[...] = tile

    def place(lo, c):
        return tiles.at[lo % 2 * 2 + c, lo // 2]

    @pl.when(native)
    def _():
        tiles[z_lo % 2 * 2 + core, z_lo // 2] = tile

    few = 2 * X + 2 * Y - 2 - (X + Y) + Z_LO
    many = few + Z_LO
    beyond = jnp.maximum(0, jnp.maximum(Z_LO - 1 - REACH - z_lo, z_lo - REACH))
    pl.semaphore_wait(barrier, jnp.where(low, few, many + jnp.where(native, 0, 1)) - beyond)

    def tile_copy(o, hi, c=None):
        return remote(
            mine, place(z_lo, core), z_s.at[hi, o], z_r.at[o, core], at(lo=(z_lo + o) % Z_LO, hi=hi, c=z_hi)
        )

    def tile_wait(o, c):
        remote(mine, place((z_lo - o + Z_LO) % Z_LO, c), z_s.at[0, 0], z_r.at[o, c], partner).wait_recv()

    high = jnp.logical_not(low)
    first_side = z_lo < Z_LO - REACH

    def passed(o):
        lo = (z_lo - o + Z_LO) % Z_LO
        on = jnp.where(first_side, lo < z_lo, jnp.logical_and(z_lo >= REACH, lo > z_lo))
        return jnp.logical_and(native, on)

    def passing(fn):
        goal = jnp.where(first_side, z_lo + REACH, jnp.maximum(z_lo - REACH, 0))
        for o in range(1, Z_LO):
            lo = (z_lo - o + Z_LO) % Z_LO

            @pl.when(passed(o))
            def _():
                for c in range(2):
                    tile = place(lo, c)
                    away = (goal - lo + Z_LO) % Z_LO
                    fn(remote(tile, tile, r_s.at[o, c], z_r.at[away, c], at(lo=goal)), o, c)


    @pl.when(high)
    def _():
        for o in range(Z_LO):
            tile_copy(o, 0).start()

    for o in range(Z_LO - 1, 0, -1):
        @pl.when(near(o)[1])
        def _():
            tile_copy(o, z_hi).start()

    @pl.when(jnp.logical_not(native))
    def _():
        tile_copy(0, z_hi).start()

    def go(device):
        pl.semaphore_signal(go_sem, inc=1, device_id=device, device_id_type=MESH)

    @pl.when(jnp.logical_and(high, jnp.logical_not(native)))
    def _():
        go(at(hi=0))

    loads[3].wait()
    loads[4].wait()
    swaps = [
        remote(owner.at[core], owner.at[core], sw_s.at[0], sw_r.at[0], partner),
        remote(doc.at[core], doc.at[core], sw_s.at[1], sw_r.at[1], partner),
        remote(rows_hbm, rows.at[core], sw_s.at[2], sw_r.at[2], partner),
    ]
    for copy in swaps:
        copy.start()

    swaps[0].wait()
    swaps[1].wait()
    id_table = jnp.zeros((owners, 128), F32)
    for side in range(2):
        owner_row = owner[side]
        table = iota((owners, count), 0) == owner_row
        earlier = dot(table.astype(BF16), before[...], NN)
        rank = jnp.sum(jnp.where(table, earlier, 0.0), axis=0, keepdims=True).astype(jnp.int32)
        slot = (owner_row * 2 + side) * cap + rank
        pick[:, side * count:(side + 1) * count] = (iota((owners * 2 * cap, count), 0) == slot).astype(BF16)
        doc_side = jnp.where(table, (doc[side] + 1).astype(F32), 0.0).astype(BF16)
        lane_side = (iota((128, count), 0) == side * cap + rank).astype(BF16)
        id_table = id_table + dot(doc_side, lane_side, NT)
    id_send[...] = id_table.reshape(id_send.shape)
    own_piece = gathered.at[y, x]
    over = remote(own_piece, own_piece, p_s, p_r, at(hi=1))
    by_piece = jnp.logical_and(high, jnp.logical_not(native))

    @pl.when(by_piece)
    def _():
        over.wait_recv()

    @pl.when(jnp.logical_not(by_piece))
    def _():
        @pl.when(jnp.logical_not(native))
        def _():
            tile_wait(0, 0)
            tile_wait(0, 1)

        @pl.when(native)
        def _():
            tile_wait(0, 1 - core)

        @pl.when(native)
        def _():
            def forward(copy, o, c):
                tile_wait(o, c)
                copy.start()

            passing(forward)

        for o in range(1, Z_LO):
            @pl.when(jnp.logical_not(passed(o)))
            def _():
                for c in range(2):
                    tile_wait(o, c)
        left = [tiles[i].astype(F32).reshape(Z_LO // 2 * 8, 128).astype(BF16) for i in range(4)]
        mixed = dot(jnp.concatenate(left, axis=1), turn[...], NN)
        for p in range(Z_LO // 2):
            part = [mixed[8 * p:8 * p + 8, 128 * j:128 * j + 128] for j in range(4)]
            for half in range(2):
                both = jnp.concatenate(part[2 * half:2 * half + 2], axis=0)
                gathered[y, x, half, :, 128 * p:128 * p + 128] = both.astype(BF16)

    def piece(dx, dy, half):
        return gathered.at[(y - dy + Y) % Y, (x - dx + X) % X, half]

    sizes = ((X, Y), (Y, X))

    def first_copy(half, j):
        device = at(dx=j) if half == 0 else at(dy=j)
        own = piece(0, 0, half)
        return remote(own, own, f_s.at[half, j], f_r.at[half, j], device)

    def second_copy(half, i, j):
        part = piece(i, 0, half) if half == 0 else piece(0, i, half)
        device = at(dy=j) if half == 0 else at(dx=j)
        return remote(part, part, g_s.at[half, i, j], g_r.at[half, i, j], device)

    copies = []

    def begin(copy):
        copy.start()
        copies.append(copy)

    for j in (2, 1, 3):
        for half in range(2):
            if j < sizes[half][0]:
                begin(first_copy(half, j))
    for i in (0, 1, 3, 2):
        for half in range(2):
            if i >= sizes[half][0]:
                continue
            if i:
                first_copy(half, i).wait_recv()
            for j in (2, 1, 3):
                if j < sizes[half][1]:
                    begin(second_copy(half, i, j))
        if i == 0:
            @pl.when(jnp.logical_and(low, native))
            def _():
                pl.semaphore_wait(go_sem, 1)
                over.start()

    def id_copy(other):
        return remote(id_send.at[other], id_got.at[chip], i_s, i_r.at[0], {"docs": other, "blk": b})

    mate = d + 1 - 2 * core
    mate_ids = remote(id_send.at[mate], id_got.at[chip], i_s, i_r.at[1], partner)

    def score_copy(other):
        return remote(
            send.at[other], got.at[core, chip], a_s, a_r.at[core], {"docs": other, "blk": b}
        )

    def settle(ref, sem):
        pltpu.make_async_copy(ref, ref, sem).wait()

    columns = [(x + dx) % X * Z_LO * 2 for dx in range(X)]

    def others(fn):
        def step(turn_no, carry):
            to = turn_no % 2 * (Z_LO // 2) + turn_no // 2

            @pl.when(to != z_lo)
            def _():
                for e in range(2):
                    fn(columns[0] + 2 * to + e)

            for dx in range(1, X):
                for e in range(2):
                    fn(columns[dx] + 2 * to + e)
            return carry

        lax.fori_loop(0, Z_LO, step, 0)

    own_ids = pltpu.make_async_copy(id_send.at[d], id_got.at[chip], loc_sem.at[6])

    @pl.when(native)
    def _():
        others(lambda other: id_copy(other).start())
        mate_ids.start()
        own_ids.start()

    loads[2].wait()
    swaps[2].wait()
    span = gathered.shape[4]
    sums = [None, None]
    for i in (0, 1, 3, 2):
        if i >= X:
            continue
        for j in range(1, Y):
            second_copy(0, i, j).wait_recv()
        for j in range(Y if i else 0):
            second_copy(1, j, i).wait_recv()
        at_x = (x - i + X) % X
        right = gathered[:, at_x].reshape(-1, span)
        for side in range(2):
            term = dot(rows[side, :, pl.ds(pl.multiple_of(at_x * span, span), span)], right, NT)
            sums[side] = term if sums[side] is None else sums[side] + term
    part = jnp.concatenate([total.astype(BF16) for total in sums], axis=0)
    send[...] = dot(pick[...], part, NN).astype(BF16).reshape(send.shape)

    @pl.when(native)
    def _():
        own_ids.wait()

    @pl.when(jnp.logical_not(native))
    def _():
        mate_ids.wait_recv()

    others(lambda other: score_copy(other).start())
    score_copy(mate).start()
    own_scores = pltpu.make_async_copy(send.at[d], got.at[core, chip], a_r.at[core])
    own_scores.start()

    settle(id_got.at[pl.ds(0, chips - 1)], i_r.at[0])
    per = chips * 2 * cap
    spread = (iota((per, chips), 0) // (2 * cap) == iota((per, chips), 1)).astype(BF16)
    ids = dot(spread, id_got[...].reshape(chips, 128).astype(BF16), NN)
    keep = iota(ids.shape, 1) == iota(ids.shape, 0) % (2 * cap)
    column = jnp.sum(jnp.where(keep, ids, 0.0), axis=1, keepdims=True).astype(jnp.int32) - 1
    member = (column == iota((per, weight.shape[1]), 1)).astype(BF16)
    loads[5].wait()

    @pl.when(high)
    def _():
        for o in range(Z_LO):
            tile_copy(o, 0).wait_send()

    for o in range(1, Z_LO):
        @pl.when(near(o)[1])
        def _():
            tile_copy(o, z_hi).wait_send()

    @pl.when(native)
    def _():
        passing(lambda copy, o, c: copy.wait_send())

    @pl.when(jnp.logical_not(native))
    def _():
        tile_copy(0, z_hi).wait_send()

    @pl.when(native)
    def _():
        settle(id_send.at[pl.ds(0, owners - 1)], i_s)

    @pl.when(jnp.logical_and(low, native))
    def _():
        over.wait_send()

    for copy in copies:
        copy.wait_send()
    for first in range(2):
        c = z_hi if first == 0 else 1 - z_hi
        if first:
            settle(send.at[pl.ds(0, owners - 1)], a_s)
        settle(got.at[c], a_r.at[c])
        total = dot(got[c].reshape(per, -1), member, TN) * weight[...]
        size = total.shape[0] // Y
        for k in range(Y):
            for nh in range(2):
                out_ref[k, c, pl.ds(nh, size, stride=2), :] = total[k * size:(k + 1) * size, nh * 128:nh * 128 + 128]


def shards(group_rows, group_owner, group_doc, doc_weight, queries, precond):
    rows = group_rows[0]
    count, width = rows.shape
    docs, blks = lax.axis_size("docs"), lax.axis_size("blk")
    chips = X * Z_LO
    cap = 2 * count // docs
    own_q, part = queries.shape[0], precond.shape[1]
    doc_count = doc_weight.shape[1]
    dma = pltpu.SemaphoreType.DMA
    any_spec = pl.BlockSpec(memory_space=pl.ANY)
    vmem = pl.BlockSpec(memory_space=pltpu.VMEM)
    nx = max(X, Y)
    total = pl.pallas_call(
        kernel,
        out_shape=pltpu.VMEM((Y, 2, 2 * own_q, doc_count // 2), F32),
        in_specs=[any_spec] * 6,
        out_specs=vmem,
        scratch_shapes=[
            pltpu.VMEM((2, count, width), BF16),
            pltpu.VMEM((2, 1, count), jnp.int32),
            pltpu.VMEM((2, 1, count), jnp.int32),
            pltpu.VMEM((1, doc_count), F32),
            pltpu.VMEM(queries.shape, BF16),
            pltpu.VMEM((part, width), BF16),
            pltpu.VMEM((8, 128), BF16),
            pltpu.VMEM((4, Z_LO // 2, 8, 128), BF16),
            pltpu.VMEM((Y, X, 2, own_q // 2, width // X), BF16),
            pltpu.VMEM((docs * 2 * cap, 2 * count), BF16),
            pltpu.VMEM((docs, 1, 128), F32),
            pltpu.VMEM((chips, 1, 128), F32),
            pltpu.VMEM((docs, 2 * cap, Y * own_q), BF16),
            pltpu.VMEM((2, chips, 2 * cap, Y * own_q), BF16),
            pltpu.VMEM((count, count), BF16),
            pltpu.VMEM((512, 512), BF16),
            dma((7,)), pltpu.SemaphoreType.REGULAR, dma((3,)), dma((3,)),
            dma((2, Z_LO)), dma((Z_LO, 2)), dma((Z_LO, 2)), dma((2, nx)), dma((2, nx)), dma((2, nx, nx)), dma((2, nx, nx)), dma, dma,
            dma, dma((2,)), dma, dma((2,)),
        ],
        compiler_params=pltpu.CompilerParams(collective_id=0, has_side_effects=True),
    )(rows, group_owner.reshape(1, count), group_doc, doc_weight, queries, precond.T)
    return total.reshape(blks * own_q, 1, doc_count)


def solution(mesh):
    return jax.shard_map(
        shards,
        mesh=mesh,
        in_specs=(
            P("blk", "docs", None),
            P("blk", "docs", None),
            P("blk", "docs"),
            P("blk", "docs"),
            P("blk", None),
            P(None, "docs"),
        ),
        out_specs=P(None, "blk", "docs"),
        check_vma=False,
    )
```

```python
import jax
import jax.numpy as jnp
from jax import lax
from jax.experimental import pallas as pl
from jax.experimental.pallas import tpu as pltpu
from jax.sharding import PartitionSpec as P

X, Y, Z_LO, Z_HI = 4, 4, 8, 2
REACH = 4
MESH = pl.DeviceIdType.MESH
NN = (((1,), (0,)), ((), ()))
NT = (((1,), (1,)), ((), ()))
TN = (((0,), (0,)), ((), ()))
F32, BF16 = jnp.float32, jnp.bfloat16


def dot(a, b, dims):
    return lax.dot_general(a, b, dims, preferred_element_type=F32)


def iota(shape, axis):
    return lax.broadcasted_iota(jnp.int32, shape, axis)


def kernel(
    rows_hbm, owner_hbm, doc_hbm, weight_hbm, query_hbm, pre_hbm, out_ref,
    rows, owner, doc, weight, query, pre, mine, tiles, gathered, pick,
    id_send, id_got, send, got, before, turn,
    loc_sem, go_sem, sw_s, sw_r, z_s, z_r, r_s, f_s, f_r, g_s, g_r, p_s, p_r,
    i_s, i_r, a_s, a_r,
):
    chips = X * Z_LO
    count = rows.shape[1]
    owners = 2 * chips
    cap = 2 * count // owners
    d, b = lax.axis_index("docs"), lax.axis_index("blk")
    core, chip = d % 2, d // 2
    x, z_lo = chip // Z_LO, chip % Z_LO
    y, z_hi = b // Z_HI, b % Z_HI
    native = core == z_hi
    low = z_hi == 0

    def at(dx=0, dy=0, lo=None, hi=None, c=None):
        lo, hi, c = (z_lo if lo is None else lo), (z_hi if hi is None else hi), (core if c is None else c)
        return {"docs": ((x + dx) % X * Z_LO + lo) * 2 + c, "blk": (y + dy) % Y * Z_HI + hi}

    def remote(src, dst, s, r, device):
        return pltpu.make_async_remote_copy(
            src_ref=src, dst_ref=dst, send_sem=s, recv_sem=r, device_id=device, device_id_type=MESH
        )

    loads = [
        pltpu.make_async_copy(src, dst, loc_sem.at[i])
        for i, (src, dst) in enumerate(
            [
                (query_hbm, query), (pre_hbm, pre), (rows_hbm, rows.at[core]),
                (owner_hbm, owner.at[core]), (doc_hbm, doc.at[core]), (weight_hbm, weight),
            ]
        )
    ]
    for copy in loads:
        copy.start()

    barrier = pltpu.get_barrier_semaphore()

    def greet(device):
        pl.semaphore_signal(barrier, inc=1, device_id=device, device_id_type=MESH)

    partner = at(c=1 - core)

    def near(o):
        lo = (z_lo + o) % Z_LO
        return lo, jnp.abs(lo - z_lo) <= REACH

    def sends(o):
        lo, close = near(o)
        return jnp.logical_or(close, jnp.logical_and(low, lo < z_lo))

    @pl.when(native)
    def _():
        for o in range(1, Z_LO):
            lo, close = near(o)

            @pl.when(jnp.logical_or(close, jnp.logical_and(low, lo > z_lo)))
            def _():
                for c in range(2):
                    greet(at(lo=lo, c=c))

        greet(partner)

    @pl.when(jnp.logical_not(native))
    def _():
        greet(partner)

    @pl.when(jnp.logical_and(low, native))
    def _():
        greet(at(hi=1))

    @pl.when(jnp.logical_and(low, jnp.logical_not(native)))
    def _():
        for o in range(Z_LO):
            for c in range(2):
                greet(at(lo=(z_lo + o) % Z_LO, hi=1, c=c))

    for j in range(1, X):
        greet(at(dx=j))
    for j in range(1, Y):
        greet(at(dy=j))

    before[...] = (iota((count, count), 0) < iota((count, count), 1)).astype(BF16)
    n = 4 * 128
    row, col = iota((n, n), 0), iota((n, n), 1)
    placed = (row // 128 == col % 128 // 32) & (row % 128 // 32 == col // 128) & (row % 32 == col % 32)
    turn[...] = placed.astype(BF16)

    loads[0].wait()
    loads[1].wait()
    block = dot(query[...], jnp.concatenate([pre[...]] * 4, axis=0), NT)
    group = iota((8, 128), 1) // 32
    tile = jnp.zeros((8, 128), F32)
    for j in range(4):
        tile = jnp.where(group == j, block[8 * j:8 * j + 8], tile)
    tile = tile.astype(BF16)
    mine[...] = tile

    def place(lo, c):
        return tiles.at[lo % 2 * 2 + c, lo // 2]

    @pl.when(native)
    def _():
        tiles[z_lo % 2 * 2 + core, z_lo // 2] = tile

    few = 2 * X + 2 * Y - 2 - (X + Y) + Z_LO
    many = few + Z_LO
    beyond = jnp.maximum(0, jnp.maximum(Z_LO - 1 - REACH - z_lo, jnp.where(low, 0, z_lo - REACH)))
    pl.semaphore_wait(barrier, jnp.where(low, few, many + jnp.where(native, 0, 1)) - beyond)

    def tile_copy(o, hi, c=None):
        return remote(
            mine, place(z_lo, core), z_s.at[hi, o], z_r.at[o, core], at(lo=(z_lo + o) % Z_LO, hi=hi, c=z_hi)
        )

    def tile_wait(o, c):
        remote(mine, place((z_lo - o + Z_LO) % Z_LO, c), z_s.at[0, 0], z_r.at[o, c], partner).wait_recv()

    high = jnp.logical_not(low)
    first_side = z_lo < Z_LO - REACH

    def passed(o):
        lo = (z_lo - o + Z_LO) % Z_LO
        on = jnp.where(first_side, lo < z_lo, jnp.logical_and(jnp.logical_and(high, z_lo >= REACH), lo > z_lo))
        return jnp.logical_and(native, on)

    def passing(fn):
        goal = jnp.where(first_side, z_lo + REACH, jnp.maximum(z_lo - REACH, 0))
        for o in range(1, Z_LO):
            lo = (z_lo - o + Z_LO) % Z_LO

            @pl.when(passed(o))
            def _():
                for c in range(2):
                    tile = place(lo, c)
                    away = (goal - lo + Z_LO) % Z_LO
                    fn(remote(tile, tile, r_s.at[o, c], z_r.at[away, c], at(lo=goal)), o, c)


    @pl.when(high)
    def _():
        for o in range(Z_LO):
            tile_copy(o, 0).start()

    for o in range(Z_LO - 1, 0, -1):
        @pl.when(sends(o))
        def _():
            tile_copy(o, z_hi).start()

    @pl.when(jnp.logical_not(native))
    def _():
        tile_copy(0, z_hi).start()

    def go(device):
        pl.semaphore_signal(go_sem, inc=1, device_id=device, device_id_type=MESH)

    @pl.when(jnp.logical_and(high, jnp.logical_not(native)))
    def _():
        go(at(hi=0))

    loads[3].wait()
    loads[4].wait()
    swaps = [
        remote(owner.at[core], owner.at[core], sw_s.at[0], sw_r.at[0], partner),
        remote(doc.at[core], doc.at[core], sw_s.at[1], sw_r.at[1], partner),
        remote(rows_hbm, rows.at[core], sw_s.at[2], sw_r.at[2], partner),
    ]
    for copy in swaps:
        copy.start()

    swaps[0].wait()
    swaps[1].wait()
    id_table = jnp.zeros((owners, 128), F32)
    for side in range(2):
        owner_row = owner[side]
        table = iota((owners, count), 0) == owner_row
        earlier = dot(table.astype(BF16), before[...], NN)
        rank = jnp.sum(jnp.where(table, earlier, 0.0), axis=0, keepdims=True).astype(jnp.int32)
        slot = (owner_row * 2 + side) * cap + rank
        pick[:, side * count:(side + 1) * count] = (iota((owners * 2 * cap, count), 0) == slot).astype(BF16)
        doc_side = jnp.where(table, (doc[side] + 1).astype(F32), 0.0).astype(BF16)
        lane_side = (iota((128, count), 0) == side * cap + rank).astype(BF16)
        id_table = id_table + dot(doc_side, lane_side, NT)
    id_send[...] = id_table.reshape(id_send.shape)
    own_piece = gathered.at[y, x]
    over = remote(own_piece, own_piece, p_s, p_r, at(hi=1))
    by_piece = jnp.logical_and(high, jnp.logical_not(native))

    @pl.when(by_piece)
    def _():
        over.wait_recv()

    @pl.when(jnp.logical_not(by_piece))
    def _():
        @pl.when(jnp.logical_not(native))
        def _():
            tile_wait(0, 0)
            tile_wait(0, 1)

        @pl.when(native)
        def _():
            tile_wait(0, 1 - core)

        @pl.when(native)
        def _():
            def forward(copy, o, c):
                tile_wait(o, c)
                copy.start()

            passing(forward)

        for o in range(1, Z_LO):
            @pl.when(jnp.logical_not(passed(o)))
            def _():
                for c in range(2):
                    tile_wait(o, c)
        left = [tiles[i].astype(F32).reshape(Z_LO // 2 * 8, 128).astype(BF16) for i in range(4)]
        mixed = dot(jnp.concatenate(left, axis=1), turn[...], NN)
        for p in range(Z_LO // 2):
            part = [mixed[8 * p:8 * p + 8, 128 * j:128 * j + 128] for j in range(4)]
            for half in range(2):
                both = jnp.concatenate(part[2 * half:2 * half + 2], axis=0)
                gathered[y, x, half, :, 128 * p:128 * p + 128] = both.astype(BF16)

    def piece(dx, dy, half):
        return gathered.at[(y - dy + Y) % Y, (x - dx + X) % X, half]

    sizes = ((X, Y), (Y, X))

    def first_copy(half, j):
        device = at(dx=j) if half == 0 else at(dy=j)
        own = piece(0, 0, half)
        return remote(own, own, f_s.at[half, j], f_r.at[half, j], device)

    def second_copy(half, i, j):
        part = piece(i, 0, half) if half == 0 else piece(0, i, half)
        device = at(dy=j) if half == 0 else at(dx=j)
        return remote(part, part, g_s.at[half, i, j], g_r.at[half, i, j], device)

    copies = []

    def begin(copy):
        copy.start()
        copies.append(copy)

    for j in (2, 1, 3):
        for half in range(2):
            if j < sizes[half][0]:
                begin(first_copy(half, j))
    for i in (0, 1, 3, 2):
        for half in range(2):
            if i >= sizes[half][0]:
                continue
            if i:
                first_copy(half, i).wait_recv()
            for j in (2, 1, 3):
                if j < sizes[half][1]:
                    begin(second_copy(half, i, j))
        if i == 0:
            @pl.when(jnp.logical_and(low, native))
            def _():
                pl.semaphore_wait(go_sem, 1)
                over.start()

    def id_copy(other):
        return remote(id_send.at[other], id_got.at[chip], i_s, i_r.at[0], {"docs": other, "blk": b})

    mate = d + 1 - 2 * core
    mate_ids = remote(id_send.at[mate], id_got.at[chip], i_s, i_r.at[1], partner)

    def score_copy(other):
        return remote(
            send.at[other], got.at[core, chip], a_s, a_r.at[core], {"docs": other, "blk": b}
        )

    def settle(ref, sem):
        pltpu.make_async_copy(ref, ref, sem).wait()

    columns = [(x + dx) % X * Z_LO * 2 for dx in range(X)]

    def others(fn):
        def step(turn_no, carry):
            to = turn_no % 2 * (Z_LO // 2) + turn_no // 2

            @pl.when(to != z_lo)
            def _():
                for e in range(2):
                    fn(columns[0] + 2 * to + e)

            for dx in range(1, X):
                for e in range(2):
                    fn(columns[dx] + 2 * to + e)
            return carry

        lax.fori_loop(0, Z_LO, step, 0)

    own_ids = pltpu.make_async_copy(id_send.at[d], id_got.at[chip], loc_sem.at[6])

    @pl.when(native)
    def _():
        others(lambda other: id_copy(other).start())
        mate_ids.start()
        own_ids.start()

    loads[2].wait()
    swaps[2].wait()
    span = gathered.shape[4]
    sums = [None, None]
    for i in (0, 1, 3, 2):
        if i >= X:
            continue
        for j in range(1, Y):
            second_copy(0, i, j).wait_recv()
        for j in range(Y if i else 0):
            second_copy(1, j, i).wait_recv()
        at_x = (x - i + X) % X
        right = gathered[:, at_x].reshape(-1, span)
        for side in range(2):
            term = dot(rows[side, :, pl.ds(pl.multiple_of(at_x * span, span), span)], right, NT)
            sums[side] = term if sums[side] is None else sums[side] + term
    part = jnp.concatenate([total.astype(BF16) for total in sums], axis=0)
    send[...] = dot(pick[...], part, NN).astype(BF16).reshape(send.shape)

    @pl.when(native)
    def _():
        own_ids.wait()

    @pl.when(jnp.logical_not(native))
    def _():
        mate_ids.wait_recv()

    others(lambda other: score_copy(other).start())
    score_copy(mate).start()
    own_scores = pltpu.make_async_copy(send.at[d], got.at[core, chip], a_r.at[core])
    own_scores.start()

    settle(id_got.at[pl.ds(0, chips - 1)], i_r.at[0])
    per = chips * 2 * cap
    spread = (iota((per, chips), 0) // (2 * cap) == iota((per, chips), 1)).astype(BF16)
    ids = dot(spread, id_got[...].reshape(chips, 128).astype(BF16), NN)
    keep = iota(ids.shape, 1) == iota(ids.shape, 0) % (2 * cap)
    column = jnp.sum(jnp.where(keep, ids, 0.0), axis=1, keepdims=True).astype(jnp.int32) - 1
    member = (column == iota((per, weight.shape[1]), 1)).astype(BF16)
    loads[5].wait()

    @pl.when(high)
    def _():
        for o in range(Z_LO):
            tile_copy(o, 0).wait_send()

    for o in range(1, Z_LO):
        @pl.when(sends(o))
        def _():
            tile_copy(o, z_hi).wait_send()

    @pl.when(native)
    def _():
        passing(lambda copy, o, c: copy.wait_send())

    @pl.when(jnp.logical_not(native))
    def _():
        tile_copy(0, z_hi).wait_send()

    @pl.when(native)
    def _():
        settle(id_send.at[pl.ds(0, owners - 1)], i_s)

    @pl.when(jnp.logical_and(low, native))
    def _():
        over.wait_send()

    for copy in copies:
        copy.wait_send()
    for first in range(2):
        c = z_hi if first == 0 else 1 - z_hi
        if first:
            settle(send.at[pl.ds(0, owners - 1)], a_s)
        settle(got.at[c], a_r.at[c])
        total = dot(got[c].reshape(per, -1), member, TN) * weight[...]
        size = total.shape[0] // Y
        for k in range(Y):
            for nh in range(2):
                out_ref[k, c, pl.ds(nh, size, stride=2), :] = total[k * size:(k + 1) * size, nh * 128:nh * 128 + 128]


def shards(group_rows, group_owner, group_doc, doc_weight, queries, precond):
    rows = group_rows[0]
    count, width = rows.shape
    docs, blks = lax.axis_size("docs"), lax.axis_size("blk")
    chips = X * Z_LO
    cap = 2 * count // docs
    own_q, part = queries.shape[0], precond.shape[1]
    doc_count = doc_weight.shape[1]
    dma = pltpu.SemaphoreType.DMA
    any_spec = pl.BlockSpec(memory_space=pl.ANY)
    vmem = pl.BlockSpec(memory_space=pltpu.VMEM)
    nx = max(X, Y)
    total = pl.pallas_call(
        kernel,
        out_shape=pltpu.VMEM((Y, 2, 2 * own_q, doc_count // 2), F32),
        in_specs=[any_spec] * 6,
        out_specs=vmem,
        scratch_shapes=[
            pltpu.VMEM((2, count, width), BF16),
            pltpu.VMEM((2, 1, count), jnp.int32),
            pltpu.VMEM((2, 1, count), jnp.int32),
            pltpu.VMEM((1, doc_count), F32),
            pltpu.VMEM(queries.shape, BF16),
            pltpu.VMEM((part, width), BF16),
            pltpu.VMEM((8, 128), BF16),
            pltpu.VMEM((4, Z_LO // 2, 8, 128), BF16),
            pltpu.VMEM((Y, X, 2, own_q // 2, width // X), BF16),
            pltpu.VMEM((docs * 2 * cap, 2 * count), BF16),
            pltpu.VMEM((docs, 1, 128), F32),
            pltpu.VMEM((chips, 1, 128), F32),
            pltpu.VMEM((docs, 2 * cap, Y * own_q), BF16),
            pltpu.VMEM((2, chips, 2 * cap, Y * own_q), BF16),
            pltpu.VMEM((count, count), BF16),
            pltpu.VMEM((512, 512), BF16),
            dma((7,)), pltpu.SemaphoreType.REGULAR, dma((3,)), dma((3,)),
            dma((2, Z_LO)), dma((Z_LO, 2)), dma((Z_LO, 2)), dma((2, nx)), dma((2, nx)), dma((2, nx, nx)), dma((2, nx, nx)), dma, dma,
            dma, dma((2,)), dma, dma((2,)),
        ],
        compiler_params=pltpu.CompilerParams(collective_id=0, has_side_effects=True),
    )(rows, group_owner.reshape(1, count), group_doc, doc_weight, queries, precond.T)
    return total.reshape(blks * own_q, 1, doc_count)


def solution(mesh):
    return jax.shard_map(
        shards,
        mesh=mesh,
        in_specs=(
            P("blk", "docs", None),
            P("blk", "docs", None),
            P("blk", "docs"),
            P("blk", "docs"),
            P("blk", None),
            P(None, "docs"),
        ),
        out_specs=P(None, "blk", "docs"),
        check_vma=False,
    )
```

```python
import jax
import jax.numpy as jnp
from jax import lax
from jax.experimental import pallas as pl
from jax.experimental.pallas import tpu as pltpu
from jax.sharding import PartitionSpec as P

X, Y, Z_LO, Z_HI = 4, 4, 8, 2
REACH = 4
MESH = pl.DeviceIdType.MESH
NN = (((1,), (0,)), ((), ()))
NT = (((1,), (1,)), ((), ()))
TN = (((0,), (0,)), ((), ()))
F32, BF16 = jnp.float32, jnp.bfloat16


def dot(a, b, dims):
    return lax.dot_general(a, b, dims, preferred_element_type=F32)


def iota(shape, axis):
    return lax.broadcasted_iota(jnp.int32, shape, axis)


def kernel(
    rows_hbm, owner_hbm, doc_hbm, weight_hbm, query_hbm, pre_hbm, out_ref,
    rows, owner, doc, weight, query, pre, mine, tiles, gathered, pick,
    id_send, id_got, send, got, before, turn,
    loc_sem, go_sem, sw_s, sw_r, z_s, z_r, r_s, f_s, f_r, g_s, g_r, p_s, p_r,
    i_s, i_r, a_s, a_r,
):
    chips = X * Z_LO
    count = rows.shape[1]
    owners = 2 * chips
    cap = 2 * count // owners
    d, b = lax.axis_index("docs"), lax.axis_index("blk")
    core, chip = d % 2, d // 2
    x, z_lo = chip // Z_LO, chip % Z_LO
    y, z_hi = b // Z_HI, b % Z_HI
    native = core == z_hi
    low = z_hi == 0

    def at(dx=0, dy=0, lo=None, hi=None, c=None):
        lo, hi, c = (z_lo if lo is None else lo), (z_hi if hi is None else hi), (core if c is None else c)
        return {"docs": ((x + dx) % X * Z_LO + lo) * 2 + c, "blk": (y + dy) % Y * Z_HI + hi}

    def remote(src, dst, s, r, device):
        return pltpu.make_async_remote_copy(
            src_ref=src, dst_ref=dst, send_sem=s, recv_sem=r, device_id=device, device_id_type=MESH
        )

    loads = [
        pltpu.make_async_copy(src, dst, loc_sem.at[i])
        for i, (src, dst) in enumerate(
            [
                (query_hbm, query), (pre_hbm, pre), (rows_hbm, rows.at[core]),
                (owner_hbm, owner.at[core]), (doc_hbm, doc.at[core]), (weight_hbm, weight),
            ]
        )
    ]
    for copy in loads:
        copy.start()

    barrier = pltpu.get_barrier_semaphore()

    def greet(device):
        pl.semaphore_signal(barrier, inc=1, device_id=device, device_id_type=MESH)

    partner = at(c=1 - core)

    def near(o):
        lo = (z_lo + o) % Z_LO
        return lo, jnp.abs(lo - z_lo) <= REACH

    @pl.when(native)
    def _():
        for o in range(1, Z_LO):
            lo, close = near(o)

            @pl.when(close)
            def _():
                for c in range(2):
                    greet(at(lo=lo, c=c))

        greet(partner)

    @pl.when(jnp.logical_not(native))
    def _():
        greet(partner)

    @pl.when(jnp.logical_and(low, native))
    def _():
        greet(at(hi=1))

    @pl.when(jnp.logical_and(low, jnp.logical_not(native)))
    def _():
        for o in range(Z_LO):
            for c in range(2):
                greet(at(lo=(z_lo + o) % Z_LO, hi=1, c=c))

    for j in range(1, X):
        greet(at(dx=j))
    for j in range(1, Y):
        greet(at(dy=j))

    before[...] = (iota((count, count), 0) < iota((count, count), 1)).astype(BF16)
    n = 4 * 128
    row, col = iota((n, n), 0), iota((n, n), 1)
    placed = (row // 128 == col % 128 // 32) & (row % 128 // 32 == col // 128) & (row % 32 == col % 32)
    turn[...] = placed.astype(BF16)

    loads[0].wait()
    loads[1].wait()
    block = dot(query[...], jnp.concatenate([pre[...]] * 4, axis=0), NT)
    group = iota((8, 128), 1) // 32
    tile = jnp.zeros((8, 128), F32)
    for j in range(4):
        tile = jnp.where(group == j, block[8 * j:8 * j + 8], tile)
    tile = tile.astype(BF16)
    mine[...] = tile

    def place(lo, c):
        return tiles.at[lo % 2 * 2 + c, lo // 2]

    @pl.when(native)
    def _():
        tiles[z_lo % 2 * 2 + core, z_lo // 2] = tile

    few = 2 * X + 2 * Y - 2 - (X + Y) + Z_LO
    many = few + Z_LO
    beyond = jnp.maximum(0, jnp.maximum(Z_LO - 1 - REACH - z_lo, z_lo - REACH))
    pl.semaphore_wait(barrier, jnp.where(low, few, many + jnp.where(native, 0, 1)) - beyond)

    def tile_copy(o, hi, c=None):
        return remote(
            mine, place(z_lo, core), z_s.at[hi, o], z_r.at[o, core], at(lo=(z_lo + o) % Z_LO, hi=hi, c=z_hi)
        )

    def tile_wait(o, c):
        remote(mine, place((z_lo - o + Z_LO) % Z_LO, c), z_s.at[0, 0], z_r.at[o, c], partner).wait_recv()

    high = jnp.logical_not(low)
    first_side = z_lo < Z_LO - REACH

    def passed(o):
        lo = (z_lo - o + Z_LO) % Z_LO
        on = jnp.where(first_side, lo < z_lo, jnp.logical_and(z_lo >= REACH, lo > z_lo))
        return jnp.logical_and(native, on)

    def passing(fn):
        goal = jnp.where(first_side, z_lo + REACH, jnp.maximum(z_lo - REACH, 0))
        for o in range(1, Z_LO):
            lo = (z_lo - o + Z_LO) % Z_LO

            @pl.when(passed(o))
            def _():
                for c in range(2):
                    tile = place(lo, c)
                    away = (goal - lo + Z_LO) % Z_LO
                    fn(remote(tile, tile, r_s.at[o, c], z_r.at[away, c], at(lo=goal)), o, c)


    @pl.when(high)
    def _():
        for o in range(Z_LO):
            tile_copy(o, 0).start()

    for o in range(Z_LO - 1, 0, -1):
        @pl.when(near(o)[1])
        def _():
            tile_copy(o, z_hi).start()

    @pl.when(jnp.logical_not(native))
    def _():
        tile_copy(0, z_hi).start()

    def go(device):
        pl.semaphore_signal(go_sem, inc=1, device_id=device, device_id_type=MESH)

    @pl.when(jnp.logical_and(high, jnp.logical_not(native)))
    def _():
        go(at(hi=0))

    loads[3].wait()
    loads[4].wait()
    swaps = [
        remote(owner.at[core], owner.at[core], sw_s.at[0], sw_r.at[0], partner),
        remote(doc.at[core], doc.at[core], sw_s.at[1], sw_r.at[1], partner),
        remote(rows_hbm, rows.at[core], sw_s.at[2], sw_r.at[2], partner),
    ]
    for copy in swaps:
        copy.start()

    swaps[0].wait()
    swaps[1].wait()
    id_table = jnp.zeros((owners, 128), F32)
    for side in range(2):
        owner_row = owner[side]
        table = iota((owners, count), 0) == owner_row
        earlier = dot(table.astype(BF16), before[...], NN)
        rank = jnp.sum(jnp.where(table, earlier, 0.0), axis=0, keepdims=True).astype(jnp.int32)
        slot = (owner_row * 2 + side) * cap + rank
        pick[:, side * count:(side + 1) * count] = (iota((owners * 2 * cap, count), 0) == slot).astype(BF16)
        doc_side = jnp.where(table, (doc[side] + 1).astype(F32), 0.0).astype(BF16)
        lane_side = (iota((128, count), 0) == side * cap + rank).astype(BF16)
        id_table = id_table + dot(doc_side, lane_side, NT)
    id_send[...] = id_table.reshape(id_send.shape)
    own_piece = gathered.at[y, x]
    over = remote(own_piece, own_piece, p_s, p_r, at(hi=1))
    by_piece = jnp.logical_and(high, jnp.logical_not(native))

    @pl.when(by_piece)
    def _():
        over.wait_recv()

    @pl.when(jnp.logical_not(by_piece))
    def _():
        @pl.when(jnp.logical_not(native))
        def _():
            tile_wait(0, 0)
            tile_wait(0, 1)

        @pl.when(native)
        def _():
            tile_wait(0, 1 - core)

        @pl.when(native)
        def _():
            def forward(copy, o, c):
                tile_wait(o, c)
                copy.start()

            passing(forward)

        for o in range(1, Z_LO):
            @pl.when(jnp.logical_not(passed(o)))
            def _():
                for c in range(2):
                    tile_wait(o, c)
        left = [tiles[i].astype(F32).reshape(Z_LO // 2 * 8, 128).astype(BF16) for i in range(4)]
        mixed = dot(jnp.concatenate(left, axis=1), turn[...], NN)
        for p in range(Z_LO // 2):
            part = [mixed[8 * p:8 * p + 8, 128 * j:128 * j + 128] for j in range(4)]
            for half in range(2):
                both = jnp.concatenate(part[2 * half:2 * half + 2], axis=0)
                gathered[y, x, half, :, 128 * p:128 * p + 128] = both.astype(BF16)

    def piece(dx, dy, half):
        return gathered.at[(y - dy + Y) % Y, (x - dx + X) % X, half]

    sizes = ((X, Y), (Y, X))

    def first_copy(half, j):
        device = at(dx=j) if half == 0 else at(dy=j)
        own = piece(0, 0, half)
        return remote(own, own, f_s.at[half, j], f_r.at[half, j], device)

    def second_copy(half, i, j):
        part = piece(i, 0, half) if half == 0 else piece(0, i, half)
        device = at(dy=j) if half == 0 else at(dx=j)
        return remote(part, part, g_s.at[half, i, j], g_r.at[half, i, j], device)

    copies = []

    def begin(copy):
        copy.start()
        copies.append(copy)

    for j in (2, 1, 3):
        for half in range(2):
            if j < sizes[half][0]:
                begin(first_copy(half, j))
    for i in (0, 1, 3, 2):
        for half in range(2):
            if i >= sizes[half][0]:
                continue
            if i:
                first_copy(half, i).wait_recv()
            for j in (2, 1, 3):
                if j < sizes[half][1]:
                    begin(second_copy(half, i, j))
        if i == 0:
            @pl.when(jnp.logical_and(low, native))
            def _():
                pl.semaphore_wait(go_sem, 1)
                over.start()

    def id_copy(other):
        return remote(id_send.at[other], id_got.at[chip], i_s, i_r.at[0], {"docs": other, "blk": b})

    mate = d + 1 - 2 * core
    mate_ids = remote(id_send.at[mate], id_got.at[chip], i_s, i_r.at[1], partner)

    def score_copy(other):
        return remote(
            send.at[other], got.at[core, chip], a_s, a_r.at[core], {"docs": other, "blk": b}
        )

    def settle(ref, sem):
        pltpu.make_async_copy(ref, ref, sem).wait()

    columns = [(x + dx) % X * Z_LO * 2 for dx in range(X)]

    def others(fn):
        def step(turn_no, carry):
            to = turn_no % 2 * (Z_LO // 2) + turn_no // 2

            @pl.when(to != z_lo)
            def _():
                for e in range(2):
                    fn(columns[0] + 2 * to + e)

            for dx in range(1, X):
                for e in range(2):
                    fn(columns[dx] + 2 * to + e)
            return carry

        lax.fori_loop(0, Z_LO, step, 0)

    own_ids = pltpu.make_async_copy(id_send.at[d], id_got.at[chip], loc_sem.at[6])

    @pl.when(native)
    def _():
        mate_ids.start()
        others(lambda other: id_copy(other).start())
        own_ids.start()

    loads[2].wait()
    swaps[2].wait()
    span = gathered.shape[4]
    sums = [None, None]
    for i in (0, 1, 3, 2):
        if i >= X:
            continue
        for j in range(1, Y):
            second_copy(0, i, j).wait_recv()
        for j in range(Y if i else 0):
            second_copy(1, j, i).wait_recv()
        at_x = (x - i + X) % X
        right = gathered[:, at_x].reshape(-1, span)
        for side in range(2):
            term = dot(rows[side, :, pl.ds(pl.multiple_of(at_x * span, span), span)], right, NT)
            sums[side] = term if sums[side] is None else sums[side] + term
    part = jnp.concatenate([total.astype(BF16) for total in sums], axis=0)
    send[...] = dot(pick[...], part, NN).astype(BF16).reshape(send.shape)

    @pl.when(native)
    def _():
        own_ids.wait()

    @pl.when(jnp.logical_not(native))
    def _():
        mate_ids.wait_recv()

    others(lambda other: score_copy(other).start())
    score_copy(mate).start()
    own_scores = pltpu.make_async_copy(send.at[d], got.at[core, chip], a_r.at[core])
    own_scores.start()

    settle(id_got.at[pl.ds(0, chips - 1)], i_r.at[0])
    per = chips * 2 * cap
    spread = (iota((per, chips), 0) // (2 * cap) == iota((per, chips), 1)).astype(BF16)
    ids = dot(spread, id_got[...].reshape(chips, 128).astype(BF16), NN)
    keep = iota(ids.shape, 1) == iota(ids.shape, 0) % (2 * cap)
    column = jnp.sum(jnp.where(keep, ids, 0.0), axis=1, keepdims=True).astype(jnp.int32) - 1
    member = (column == iota((per, weight.shape[1]), 1)).astype(BF16)
    loads[5].wait()

    @pl.when(high)
    def _():
        for o in range(Z_LO):
            tile_copy(o, 0).wait_send()

    for o in range(1, Z_LO):
        @pl.when(near(o)[1])
        def _():
            tile_copy(o, z_hi).wait_send()

    @pl.when(native)
    def _():
        passing(lambda copy, o, c: copy.wait_send())

    @pl.when(jnp.logical_not(native))
    def _():
        tile_copy(0, z_hi).wait_send()

    @pl.when(native)
    def _():
        settle(id_send.at[pl.ds(0, owners - 1)], i_s)

    @pl.when(jnp.logical_and(low, native))
    def _():
        over.wait_send()

    for copy in copies:
        copy.wait_send()
    for first in range(2):
        c = z_hi if first == 0 else 1 - z_hi
        if first:
            settle(send.at[pl.ds(0, owners - 1)], a_s)
        settle(got.at[c], a_r.at[c])
        total = dot(got[c].reshape(per, -1), member, TN) * weight[...]
        size = total.shape[0] // Y
        for k in range(Y):
            for nh in range(2):
                out_ref[k, c, pl.ds(nh, size, stride=2), :] = total[k * size:(k + 1) * size, nh * 128:nh * 128 + 128]


def shards(group_rows, group_owner, group_doc, doc_weight, queries, precond):
    rows = group_rows[0]
    count, width = rows.shape
    docs, blks = lax.axis_size("docs"), lax.axis_size("blk")
    chips = X * Z_LO
    cap = 2 * count // docs
    own_q, part = queries.shape[0], precond.shape[1]
    doc_count = doc_weight.shape[1]
    dma = pltpu.SemaphoreType.DMA
    any_spec = pl.BlockSpec(memory_space=pl.ANY)
    vmem = pl.BlockSpec(memory_space=pltpu.VMEM)
    nx = max(X, Y)
    total = pl.pallas_call(
        kernel,
        out_shape=pltpu.VMEM((Y, 2, 2 * own_q, doc_count // 2), F32),
        in_specs=[any_spec] * 6,
        out_specs=vmem,
        scratch_shapes=[
            pltpu.VMEM((2, count, width), BF16),
            pltpu.VMEM((2, 1, count), jnp.int32),
            pltpu.VMEM((2, 1, count), jnp.int32),
            pltpu.VMEM((1, doc_count), F32),
            pltpu.VMEM(queries.shape, BF16),
            pltpu.VMEM((part, width), BF16),
            pltpu.VMEM((8, 128), BF16),
            pltpu.VMEM((4, Z_LO // 2, 8, 128), BF16),
            pltpu.VMEM((Y, X, 2, own_q // 2, width // X), BF16),
            pltpu.VMEM((docs * 2 * cap, 2 * count), BF16),
            pltpu.VMEM((docs, 1, 128), F32),
            pltpu.VMEM((chips, 1, 128), F32),
            pltpu.VMEM((docs, 2 * cap, Y * own_q), BF16),
            pltpu.VMEM((2, chips, 2 * cap, Y * own_q), BF16),
            pltpu.VMEM((count, count), BF16),
            pltpu.VMEM((512, 512), BF16),
            dma((7,)), pltpu.SemaphoreType.REGULAR, dma((3,)), dma((3,)),
            dma((2, Z_LO)), dma((Z_LO, 2)), dma((Z_LO, 2)), dma((2, nx)), dma((2, nx)), dma((2, nx, nx)), dma((2, nx, nx)), dma, dma,
            dma, dma((2,)), dma, dma((2,)),
        ],
        compiler_params=pltpu.CompilerParams(collective_id=0, has_side_effects=True),
    )(rows, group_owner.reshape(1, count), group_doc, doc_weight, queries, precond.T)
    return total.reshape(blks * own_q, 1, doc_count)


def solution(mesh):
    return jax.shard_map(
        shards,
        mesh=mesh,
        in_specs=(
            P("blk", "docs", None),
            P("blk", "docs", None),
            P("blk", "docs"),
            P("blk", "docs"),
            P("blk", None),
            P(None, "docs"),
        ),
        out_specs=P(None, "blk", "docs"),
        check_vma=False,
    )
```
